512 devices in a mesh: lat: 64 (over z, y), ord: 2 (over core), orb: 4 (over x).
Axes of the slice: x: 4, y: 4, z: 16, core: 2. Of those that a mesh axis runs over, the one named last changes fastest.
Arguments:
- anomaly: bfloat16 [2, 1024, 4320], P(None, 'lat'), may hold values from -6 to 6
- row_weight: float32 [2, 1024], replicated, may hold values from 0.2 to 1
- panel: bfloat16 [4, 64, 1024, 2, 640], P('orb', None, 'lat', 'ord'), may hold values from -0.125 to 0.125
- order_value: int32 [4, 64], P('orb'), may hold values from 0 to 2159
- deg_first: int32 [4, 64], P('orb', 'lat'), may hold values from 0 to 2190
- sat_rows: bfloat16 [131072, 256], P(('lat', 'ord', 'orb')), may hold values from -0.25 to 0.25
- sat_slot: int32 [131072, 1], P(('lat', 'ord', 'orb')), may hold values from 0 to 255; in each aligned block of 256 rows (0 to 255, 256 to 511, ...) at most 2 rows name the same one
Outputs:
- normals: float32 [4, 64, 2, 640, 2, 640], P('orb', 'lat', 'ord')
- right_side: float32 [4, 64, 2, 2, 640], P('orb', 'lat', None, 'ord')
The draws below stay inside these ranges and needn't reach their ends.
Inputs may be any that keep to these rules, and one draw needn't show every extreme that they name: `sat_slot`: among the 256 rows of one device no order slot appears more than 2 times.
All inputs are finite; a program needn't handle non-finite values.
Results may differ from the reference program's by a relative error of at most 0.0029.
Values may be sent and summed in bfloat16 or wider, within the bound.
No kernel may reach another device: no remote copies, remote signals or barrier semaphores. Data moves between devices by JAX's collectives and lax.ppermute only.
A program may use at most 64 MiB of HBM per device.

```python
import math
import jax
import jax.numpy as jnp
import numpy as np
from jax import lax

NLON = 4320
LMAX = 2190
K = 1280
KS = 256
SAT_DEV = 256
NROWS = 1024
GROUPS = 4
GORD = 64
ORDERS = 256
CAP = 2
SAT = 131072
N_LAT = 64
N_ORD = 2
N_ORB = 4


def with_ends(result, stream_key, least, high):
    longest = result.shape.index(max(result.shape))
    spots = []
    for shift in (0, 1):
        where = [jax.random.randint(jax.random.fold_in(stream_key, axis), (), 0, length) for axis, length in enumerate(result.shape)]
        where[longest] = (where[longest] + shift) % result.shape[longest]
        spots.append(tuple(where))
    return result.at[spots[0]].set(least).at[spots[1]].set(high)


def steps_of(own_key, extent, split, least, high):
    level, own = 1.0, jax.random.fold_in(own_key, 6)
    for dim, shards_of in split:
        heights = jnp.exp(jax.random.uniform(jax.random.fold_in(own, dim), (shards_of,), jnp.float32, least / len(split), high / len(split)))
        level = level * jnp.repeat(heights, extent[dim] // shards_of).reshape([-1 if axis == dim else 1 for axis in range(len(extent))])
    return level


def routed_block(stream_key, own, number, rows, count, top, bound, skew):
    sequence = jax.random.permutation(stream_key, count)
    crowded, ordinary = shares(count, rows * top, bound, skew, True), shares(count, rows * top, bound, skew, False)
    places = jnp.arange(count)

    def named(lengths, rotation):
        used = int((lengths > 0).sum())
        fixed = max(1, used // 4)
        moved = fixed + (places - fixed + rotation * (used - fixed)) % max(1, count - fixed)
        return jnp.zeros((count,), jnp.int32).at[sequence[jnp.where(places < fixed, places, moved)]].set(jnp.asarray(lengths, jnp.int32))

    lengths = jnp.where(number % 4 == 0, named(crowded, number // 4), named(ordinary, number - number // 4 - 1))
    mixed = jax.random.permutation(jax.random.fold_in(own, 3), count)
    donor, taker = mixed[0:count // 2 * 2:2], mixed[1:count // 2 * 2:2]
    slack = jnp.minimum(lengths[donor] - 1, bound - lengths[taker]) // 2
    slack = jnp.where((donor == sequence[0]) | (taker == sequence[0]) | (lengths[taker] == 0), 0, jnp.maximum(slack, 0))
    moved = jax.random.randint(jax.random.fold_in(own, 4), (count // 2,), 0, 1 << 20) % (slack + 1)
    lengths = lengths.at[donor].add(-moved).at[taker].add(moved)
    items = jnp.searchsorted(jnp.cumsum(lengths), jnp.arange(rows * top), side="right").astype(jnp.int32)
    listing = items.reshape(top, rows).T
    listing = listing[jax.random.permutation(jax.random.fold_in(own, 1), rows)]
    rotation = jax.random.randint(jax.random.fold_in(own, 2), (rows, 1), 0, top)
    return jnp.take_along_axis(listing, (jnp.arange(top)[None, :] + rotation) % top, axis=1)


def shares(number_of, total, most, lean, full):
    weights = [(1 << 20) // math.isqrt(rank ** lean) + 1 for rank in range(1, number_of + 1)]
    largest = most if full else min(most, max(-(-total // number_of), total * weights[0] // sum(weights)))
    least = 1 if total - largest >= number_of - 1 else 0
    holding, rest = [largest] + [least] * (number_of - 1), total - largest - least * (number_of - 1)
    while rest > 0:
        movable = [i for i in range(1, number_of) if holding[i] < largest] or [i for i in range(1, number_of) if holding[i] < most]
        mass, left = sum([weights[i] for i in movable]), rest
        for i in movable:
            extra = min(most - holding[i], max(1, left * weights[i] // mass), rest)
            holding[i] = holding[i] + extra
            rest = rest - extra
    return np.array(holding)


def centred(stream_key, dims, deviation, most, split=(), kind=jnp.bfloat16):
    gain = steps_of(stream_key, dims, split, -0.22, 0.18) if split else 1.0
    array = jax.random.normal(stream_key, dims, jnp.float32) * deviation * gain
    return jnp.minimum(jnp.maximum(array, -most), most).astype(kind)


def setup_inputs(seed: int = 0) -> dict:
    key_list = jax.random.split(jax.random.key(seed), 8)
    anomaly = centred(key_list[0], (2, NROWS, NLON), 1.0, 6.0, ((1, 64),))
    row_weight = jnp.clip(jnp.exp(jax.random.uniform(key_list[1], (2, NROWS), jnp.float32, math.log(0.2), math.log(1.0))), 0.2, 1.0)
    panel = centred(key_list[2], (GROUPS, GORD, NROWS, 2, K // 2), (2 * NROWS) ** -0.5, 0.125, ((0, 4), (2, 64), (3, 2)))
    order_value = with_ends(jax.random.randint(key_list[3], (GROUPS, GORD), 0, NLON // 2), jax.random.fold_in(key_list[3], 1), 0, (NLON // 2) - 1).astype(jnp.int32)
    deg_first = with_ends(jax.random.randint(key_list[4], (GROUPS, GORD), 0, LMAX + 1), jax.random.fold_in(key_list[4], 1), 0, LMAX).astype(jnp.int32)
    sat_rows = centred(key_list[5], (SAT, KS), (SAT_DEV * N_LAT * N_ORD * N_ORB // ORDERS) ** -0.5, 0.25, ((0, 512),))
    sat_slot_keys = jax.random.split(jax.random.fold_in(key_list[6], 1), SAT // SAT_DEV)
    sat_slot_turns = jax.random.permutation(jax.random.fold_in(key_list[6], 3), SAT // SAT_DEV)
    sat_slot = jax.vmap(lambda own, number: routed_block(jax.random.fold_in(key_list[6], 2), own, number, SAT_DEV, ORDERS, 1, CAP, 2))(sat_slot_keys, sat_slot_turns).reshape((SAT, 1))
    return {"anomaly": anomaly, "row_weight": row_weight, "panel": panel, "order_value": order_value, "deg_first": deg_first, "sat_rows": sat_rows, "sat_slot": sat_slot}


def reference(anomaly, row_weight, panel, order_value, deg_first, sat_rows, sat_slot):
    half_count = K // 2
    half_sat = KS // 2
    order_flat = order_value.reshape(-1).astype(jnp.int32)
    first_flat = deg_first.reshape(-1).astype(jnp.int32)
    parity_col = jnp.arange(2, dtype=jnp.int32)[:, None] + 2 * jnp.arange(half_count, dtype=jnp.int32)[None, :]
    degree = first_flat[:, None, None] + parity_col[None]
    live_flags = (degree <= LMAX).astype(jnp.float32)
    parity_sign = 1.0 - 2.0 * ((degree + order_flat[:, None, None]) % 2).astype(jnp.float32)
    spectra = jnp.fft.rfft(anomaly.astype(jnp.float32), axis=-1)[:, :, order_flat]
    scale_factor = math.sqrt(2.0 / NLON)
    cos_part = (jnp.real(spectra) * scale_factor).astype(jnp.float32)
    sin_part = (-jnp.imag(spectra) * scale_factor).astype(jnp.float32)
    weight_north = row_weight[0][:, None]
    weight_south = row_weight[1][:, None]
    coefficients = jnp.stack([weight_north * cos_part[0], weight_north * sin_part[0], weight_south * cos_part[1], weight_south * sin_part[1]], axis=-1).astype(jnp.bfloat16)
    coefficients = jnp.transpose(coefficients, (1, 0, 2))
    panel_flat = panel.reshape(-1, NROWS, 2, half_count)
    plus_weight = (row_weight[0] + row_weight[1])[:, None, None]
    minus_weight = (row_weight[0] - row_weight[1])[:, None, None]
    device_total = N_LAT * N_ORD * N_ORB
    order_total = order_flat.shape[0]
    sat_by_device = sat_rows.reshape(device_total, SAT_DEV, KS)
    slot_by_device = sat_slot.reshape(device_total, SAT_DEV).astype(jnp.int32)
    position = jnp.arange(SAT_DEV, dtype=jnp.int32)

    def add_device(total, pieces):
        rows_one, slot_one = pieces
        earlier = (slot_one[:, None] == slot_one[None, :]) & (position[None, :] < position[:, None])
        slot_rank = lax.optimization_barrier(jnp.sum(earlier, axis=1, dtype=jnp.int32))
        target = slot_one * CAP + slot_rank
        bucket = jnp.zeros((order_total * CAP, KS), jnp.float32).at[target].set(rows_one.astype(jnp.float32))
        bucket = bucket.reshape(order_total, CAP, KS)
        return (total + jnp.einsum('ock,ocl->okl', bucket, bucket, precision=lax.Precision.HIGHEST), None)
    sat_normal, _ = lax.scan(add_device, jnp.zeros((order_total, KS, KS), jnp.float32), (sat_by_device, slot_by_device))
    sat_parity = sat_normal.reshape(order_total, half_sat, 2, half_sat, 2).transpose(0, 2, 1, 4, 3)

    def per_order(pieces):
        panel_one, live_one, sign_one, coef_one, sat_one = pieces
        masked = (panel_one.astype(jnp.float32) * live_one[None]).astype(jnp.bfloat16)
        plus_panel = (masked.astype(jnp.float32) * plus_weight).astype(jnp.bfloat16)
        minus_panel = (masked.astype(jnp.float32) * minus_weight).astype(jnp.bfloat16)
        masked_wide = masked.astype(jnp.float32)
        plus_wide = plus_panel.astype(jnp.float32)
        minus_wide = minus_panel.astype(jnp.float32)
        same_block = jnp.einsum('rpi,rpj->pij', masked_wide, plus_wide, precision=lax.Precision.HIGHEST)
        cross_block = jnp.einsum('rpi,rpj->pij', masked_wide, minus_wide[:, ::-1], precision=lax.Precision.HIGHEST)
        upper_rows = jnp.stack([same_block[0], cross_block[0]], axis=1)
        lower_rows = jnp.stack([cross_block[1], same_block[1]], axis=1)
        grid_normal = jnp.stack([upper_rows, lower_rows], axis=0)
        sat_full = jnp.pad(sat_one, ((0, 0), (0, half_count - half_sat), (0, 0), (0, half_count - half_sat)))
        normal_one = grid_normal + sat_full * (live_one[:, :, None, None] * live_one[None, None, :, :])
        products = jnp.einsum('rpi,rc->cpi', masked_wide, coef_one.astype(jnp.float32), precision=lax.Precision.HIGHEST)
        right_one = jnp.stack([products[0] + sign_one * products[2], products[1] + sign_one * products[3]])
        return (normal_one, right_one)
    normal_all, right_all = lax.map(per_order, (panel_flat, live_flags, parity_sign, coefficients, sat_parity))
    return (normal_all.reshape(GROUPS, GORD, 2, half_count, 2, half_count), right_all.reshape(GROUPS, GORD, 2, 2, half_count))
```

```python
import math

import jax
import jax.numpy as jnp
from jax import lax
from jax.experimental import pallas as pl
from jax.experimental.pallas import tpu as pltpu
from jax.sharding import PartitionSpec as P

LMAX = 2190
F32 = jnp.float32
BF16 = jnp.bfloat16
I32 = jnp.int32
STEP = 144


def iota(shape, dim):
    return lax.broadcasted_iota(I32, shape, dim)


def dot(left, right, dims):
    return lax.dot_general(left, right, (dims, ((), ())), preferred_element_type=F32)


def turn(product, length):
    whole = jnp.floor(product * (1.0 / length))
    return (product - whole * length) * (2.0 * math.pi / length)


def prepare_kernel(place, anomaly, weight, order, rows, slot, out, table_high, table_low):
    z, y, x = place[0], place[1], place[2]
    length = anomaly.shape[2]
    order_pair = jnp.concatenate([order[...], order[...]], axis=1).astype(F32)
    fine = turn(iota((STEP, 128), 0).astype(F32) * order_pair, length)
    coarse_count = length // STEP
    coarse_rows = -(-coarse_count // 8) * 8
    coarse = turn(iota((coarse_rows, 128), 0).astype(F32) * (order_pair * STEP), length)
    cos_fine, sin_fine = jnp.cos(fine), jnp.sin(fine)
    cos_coarse, sin_coarse = jnp.cos(coarse), jnp.sin(coarse)
    left = iota((coarse_rows, 128), 1) < 64
    by_cos = jnp.where(left, cos_coarse, sin_coarse)
    by_sin = jnp.where(left, -sin_coarse, cos_coarse)
    for k in range(coarse_count):
        value = by_cos[k : k + 1] * cos_fine + by_sin[k : k + 1] * sin_fine
        high = value.astype(BF16)
        table_high[k * STEP : (k + 1) * STEP] = high
        table_low[k * STEP : (k + 1) * STEP] = (value - high.astype(F32)).astype(BF16)
    samples = anomaly[...].reshape(32, length)
    spectra = dot(samples, table_high[...], ((1,), (0,))) + dot(samples, table_low[...], ((1,), (0,)))
    coef = (spectra * math.sqrt(2.0 / length) * weight[...]).astype(BF16)
    at, own = iota((64, 64), 0), iota((64, 64), 1)

    def position(slot_in_group):
        ahead = ((slot_in_group >> 2) - z) & 15
        side = ((slot_in_group & 3) - y) & 3
        near = (ahead + 1) & 3
        far = ((ahead - (near - 1)) & 15) >> 2
        return side * 16 + near * 4 + far

    pick = (position(own) == at).astype(F32).astype(BF16)
    out[:, 2048:2176] = jnp.concatenate(
        [
            dot(pick, coef[:, :64], ((1,), (1,))),
            dot(pick, coef[:, 64:], ((1,), (1,))),
            jnp.zeros((64, 64), F32),
        ],
        axis=1,
    ).astype(BF16)
    col, to = iota((256, 256), 0), iota((256, 256), 1)
    apart = ((col & 1) * 128 + (col >> 1) == to).astype(F32).astype(BF16)
    split_rows = dot(rows[...], apart, ((1,), (0,))).astype(BF16)
    slot_row = jnp.broadcast_to(slot[...], (256, 256))
    slot_col = slot_row.T
    earlier = (slot_col == slot_row) & (col < to)
    rank = jnp.sum(jnp.where(earlier, 1.0, 0.0), axis=0, keepdims=True).astype(I32)
    slot_now = slot[...]
    bucket = ((((slot_now >> 6) - x) & 3) * 2 + rank) * 64 + position(slot_now & 63)
    chosen = (jnp.broadcast_to(bucket, (512, 256)) == iota((512, 256), 0)).astype(F32).astype(BF16)
    placed = dot(chosen, split_rows, ((1,), (0,))).astype(BF16)
    for q in range(8):
        out[:, q * 256 : (q + 1) * 256] = placed[q * 64 : (q + 1) * 64]


def gather_kernel(place, sat_own, sat_other, coef, weight, sat_out, coef_out, plus_out, minus_out):
    z, y, p = place[0], place[1], place[3]
    gram = jnp.zeros((256, 256), F32)
    for part in (sat_own, sat_other):
        for c in range(2):
            block = part[:, c * 256 : (c + 1) * 256]
            gram = gram + dot(block, block, ((0,), (0,)))
    sat_out[...] = jnp.where(p == 0, gram[:128], gram[128:])
    index = iota((64, 1024), 0)
    far, near, side = index >> 4, (index >> 2) & 3, index & 3
    source = ((z - far * 4 - (near - 1)) & 15) * 4 + ((y - side) & 3)
    mine = source == (iota((64, 1024), 1) >> 4)
    spread = ((iota((16, 1024), 1) & 15) == iota((16, 1024), 0)).astype(F32).astype(BF16)
    lines = []
    for c in range(4):
        wide = dot(coef[:, c * 16 : (c + 1) * 16], spread, ((1,), (0,)))
        lines.append(jnp.sum(jnp.where(mine, wide, 0.0), axis=0, keepdims=True))
    lines.append(jnp.zeros((4, 1024), F32))
    coef_out[...] = jnp.concatenate(lines, axis=0).astype(BF16)
    plus = weight[0:1] + weight[1:2]
    minus = weight[0:1] - weight[1:2]
    plus_out[...] = jnp.broadcast_to(plus, (128, 1024)).T
    minus_out[...] = jnp.broadcast_to(minus, (128, 1024)).T


def live_row(first, parity, half):
    return (first + 2 * iota((1, half), 1) + parity <= LMAX).astype(F32)


def same_kernel(place, own, coef, plus, turned, same, right):
    p, first, order = place[3], place[4], place[5]
    half = own.shape[1]
    live = live_row(first, p, half)
    wide = own[...].astype(F32) * live
    masked = wide.astype(BF16)
    turned_now = masked.T
    turned[...] = turned_now
    scale = jnp.concatenate([plus[...]] * (half // 128), axis=1)
    same[...] = dot(turned_now, (wide * scale).astype(BF16), ((1,), (0,)))
    product = dot(coef[...], masked, ((1,), (0,)))
    sign = 1.0 - 2.0 * ((first + p + order + iota((1, half), 1) * 2) & 1).astype(F32)
    right[0:1] = product[0:1] + sign * product[1:2]
    right[1:2] = product[2:3] + sign * product[3:4]


def cross_kernel(place, turned, other, minus, same, sat, out, scaled):
    p, first = place[3], place[4]
    half = other.shape[1]
    step = pl.program_id(0)

    @pl.when(step == 0)
    def _():
        live_other = live_row(first, 1 - p, half)
        scale = jnp.concatenate([minus[...]] * (half // 128), axis=1)
        scaled[...] = (other[...].astype(F32) * live_other * scale).astype(BF16)

    cross = dot(turned[...], scaled[...], ((1,), (0,)))
    same_now = same[...]
    out[:, 0, :] = jnp.where(p == 0, same_now, cross)
    out[:, 1, :] = jnp.where(p == 0, cross, same_now)

    @pl.when(step == 0)
    def _():
        live_left = (first + 2 * iota((128, 128), 0) + p <= LMAX).astype(F32)
        for q in range(2):
            live_top = (first + 2 * iota((128, 128), 1) + q <= LMAX).astype(F32)
            add = sat[:, q * 128 : (q + 1) * 128] * (live_left * live_top)
            out[:, q, 0:128] = out[:, q, 0:128] + add


def whole(memory_space=pltpu.VMEM):
    return pl.BlockSpec(memory_space=memory_space)


def shards(anomaly, row_weight, panel, order_value, deg_first, sat_rows, sat_slot):
    lat_index = lax.axis_index("lat")
    parity = lax.axis_index("ord")
    orb_index = lax.axis_index("orb")
    row_count = panel.shape[2]
    half = panel.shape[4]
    row_all = row_weight.shape[1]
    z, y = lat_index // 4, lat_index % 4
    smem = whole(pltpu.SMEM)

    arrived = lax.all_to_all(panel, "lat", split_axis=1, concat_axis=2, tiled=True)

    own_order = lax.dynamic_slice_in_dim(order_value[0], lat_index, 1, 0)[0]
    place = jnp.stack([z, y, orb_index, parity, deg_first[0, 0], own_order]).astype(I32)
    local_weight = lax.dynamic_slice_in_dim(row_weight, lat_index * row_count, row_count, 1)
    packed = pl.pallas_call(
        prepare_kernel,
        out_shape=jax.ShapeDtypeStruct((64, 2176), BF16),
        in_specs=[smem] + [whole()] * 5,
        out_specs=whole(),
        scratch_shapes=[pltpu.VMEM((anomaly.shape[2], 128), BF16)] * 2,
        name="prepare",
    )(
        place,
        anomaly,
        local_weight.reshape(2 * row_count, 1),
        order_value,
        sat_rows,
        sat_slot.reshape(1, sat_slot.shape[0]),
    )

    def lat_shift(dz, dy):
        return [
            (a * 4 + b, (a + dz) % 16 * 4 + (b + dy) % 4) for a in range(16) for b in range(4)
        ]

    width = packed.shape[1]
    blocks = packed.reshape(4, 16, width)
    sides = [blocks[0]] + [lax.ppermute(blocks[e], "lat", lat_shift(0, e)) for e in (1, 2, 3)]
    sides = [s.reshape(4, 4, width) for s in sides]
    nears = []
    for k in range(4):
        part = jnp.stack([s[k] for s in sides])
        nears.append(part if k == 1 else lax.ppermute(part, "lat", lat_shift(k - 1, 0)))
    stacked = jnp.stack(nears).reshape(16, 4, width).transpose(1, 0, 2)
    fars = [stacked[0]]
    fars += [lax.ppermute(stacked[k], "lat", lat_shift(4 * k, 0)) for k in (1, 2, 3)]
    gathered = jnp.concatenate(fars, axis=0)
    groups = [gathered[:, :512]]
    for f in (1, 2, 3):
        groups.append(
            lax.ppermute(
                gathered[:, f * 512 : (f + 1) * 512], "orb", [(i, (i + f) % 4) for i in range(4)]
            )
        )
    sat_own = jnp.concatenate(groups, axis=0)
    sat_other = lax.ppermute(sat_own, "ord", [(0, 1), (1, 0)])

    sat_gram, coef, plus, minus = pl.pallas_call(
        gather_kernel,
        out_shape=(
            jax.ShapeDtypeStruct((128, 256), F32),
            jax.ShapeDtypeStruct((8, row_all), BF16),
            jax.ShapeDtypeStruct((row_all, 128), F32),
            jax.ShapeDtypeStruct((row_all, 128), F32),
        ),
        in_specs=[smem] + [whole()] * 4,
        out_specs=(whole(),) * 4,
        name="gather",
    )(place, sat_own, sat_other, gathered[:, 2048:], row_weight)

    own_panel = arrived.reshape(row_all, half)
    other_panel = lax.ppermute(own_panel, "ord", [(0, 1), (1, 0)])
    turned, same, right = pl.pallas_call(
        same_kernel,
        out_shape=(
            jax.ShapeDtypeStruct((half, row_all), BF16),
            jax.ShapeDtypeStruct((half, half), F32),
            jax.ShapeDtypeStruct((2, half), F32),
        ),
        in_specs=[smem] + [whole()] * 3,
        out_specs=(whole(),) * 3,
        name="same",
    )(place, own_panel, coef, plus)
    normals = pl.pallas_call(
        cross_kernel,
        grid=(half // 128,),
        out_shape=jax.ShapeDtypeStruct((half, 2, half), F32),
        in_specs=[
            smem,
            pl.BlockSpec((128, row_all), lambda i: (i, 0)),
            pl.BlockSpec((row_all, half), lambda i: (0, 0)),
            pl.BlockSpec((row_all, 128), lambda i: (0, 0)),
            pl.BlockSpec((128, half), lambda i: (i, 0)),
            pl.BlockSpec((128, 256), lambda i: (0, 0)),
        ],
        out_specs=pl.BlockSpec((128, 2, half), lambda i: (i, 0, 0)),
        scratch_shapes=[pltpu.VMEM((row_all, half), BF16)],
        name="cross",
    )(place, turned, other_panel, minus, same, sat_gram)
    return (normals[None, None, None], right[None, None, :, None, :])


def solution(mesh):
    in_specs = (
        P(None, "lat", None),
        P(),
        P("orb", None, "lat", "ord", None),
        P("orb", None),
        P("orb", "lat"),
        P(("lat", "ord", "orb"), None),
        P(("lat", "ord", "orb"), None),
    )
    out_specs = (P("orb", "lat", "ord", None, None, None), P("orb", "lat", None, "ord", None))
    return jax.shard_map(shards, mesh=mesh, in_specs=in_specs, out_specs=out_specs, check_vma=False)
```

```python
import math

import jax
import jax.numpy as jnp
from jax import lax
from jax.experimental import pallas as pl
from jax.experimental.pallas import tpu as pltpu
from jax.sharding import PartitionSpec as P


LMAX = 2190
F32 = jnp.float32
BF16 = jnp.bfloat16
I32 = jnp.int32
STEP = 144


def iota(shape, dim):
    return lax.broadcasted_iota(I32, shape, dim)


def dot(left, right, dims):
    return lax.dot_general(left, right, (dims, ((), ())), preferred_element_type=F32)


def turn(product, length):
    whole = jnp.floor(product * (1.0 / length))
    return (product - whole * length) * (2.0 * math.pi / length)


def prepare_kernel(place, anomaly, weight, order, rows, slot, out, table_high, table_low):
    y, x = place[1], place[2]
    length = anomaly.shape[2]
    order_pair = jnp.concatenate([order[...], order[...]], axis=1).astype(F32)
    fine = turn(iota((STEP, 128), 0).astype(F32) * order_pair, length)
    coarse_count = length // STEP
    coarse_rows = -(-coarse_count // 8) * 8
    coarse = turn(iota((coarse_rows, 128), 0).astype(F32) * (order_pair * STEP), length)
    cos_fine, sin_fine = jnp.cos(fine), jnp.sin(fine)
    cos_coarse, sin_coarse = jnp.cos(coarse), jnp.sin(coarse)
    left = iota((coarse_rows, 128), 1) < 64
    by_cos = jnp.where(left, cos_coarse, sin_coarse)
    by_sin = jnp.where(left, -sin_coarse, cos_coarse)
    for k in range(coarse_count):
        value = by_cos[k : k + 1] * cos_fine + by_sin[k : k + 1] * sin_fine
        high = value.astype(BF16)
        table_high[k * STEP : (k + 1) * STEP] = high
        table_low[k * STEP : (k + 1) * STEP] = (value - high.astype(F32)).astype(BF16)
    samples = anomaly[...].reshape(32, length)
    spectra = dot(samples, table_high[...], ((1,), (0,))) + dot(samples, table_low[...], ((1,), (0,)))
    coef = (spectra * math.sqrt(2.0 / length) * weight[...]).astype(BF16)
    at, own = iota((64, 64), 0), iota((64, 64), 1)

    def position(slot_in_group):
        side = ((slot_in_group & 3) - y) & 3
        return side * 16 + (slot_in_group >> 2)

    pick = (position(own) == at).astype(F32).astype(BF16)
    out[:, 2048:2176] = jnp.concatenate(
        [
            dot(pick, coef[:, :64], ((1,), (1,))),
            dot(pick, coef[:, 64:], ((1,), (1,))),
            jnp.zeros((64, 64), F32),
        ],
        axis=1,
    ).astype(BF16)
    col, to = iota((256, 256), 0), iota((256, 256), 1)
    apart = ((col & 1) * 128 + (col >> 1) == to).astype(F32).astype(BF16)
    split_rows = dot(rows[...], apart, ((1,), (0,))).astype(BF16)
    slot_row = jnp.broadcast_to(slot[...], (256, 256))
    slot_col = slot_row.T
    earlier = (slot_col == slot_row) & (col < to)
    rank = jnp.sum(jnp.where(earlier, 1.0, 0.0), axis=0, keepdims=True).astype(I32)
    slot_now = slot[...]
    bucket = ((((slot_now >> 6) - x) & 3) * 2 + rank) * 64 + position(slot_now & 63)
    chosen = (jnp.broadcast_to(bucket, (512, 256)) == iota((512, 256), 0)).astype(F32).astype(BF16)
    placed = dot(chosen, split_rows, ((1,), (0,))).astype(BF16)
    for q in range(8):
        out[:, q * 256 : (q + 1) * 256] = placed[q * 64 : (q + 1) * 64]


def gather_kernel(place, sat, coef_out, sent, kept):
    y, p = place[1], place[3]
    gram = jnp.zeros((256, 256), F32)
    for c in range(8):
        block = sat[:, c * 256 : (c + 1) * 256]
        gram = gram + dot(block, block, ((0,), (0,)))
    kept[...] = jnp.where(p == 0, gram[:128], gram[128:])
    sent[...] = jnp.where(p == 0, gram[128:], gram[:128])
    index = iota((64, 1024), 0)
    source = (index & 60) + ((y - index) & 3)
    mine = source == (iota((64, 1024), 1) >> 4)
    spread = ((iota((16, 1024), 1) & 15) == iota((16, 1024), 0)).astype(F32).astype(BF16)
    lines = []
    for c in range(4):
        wide = dot(sat[:, 2048 + c * 16 : 2048 + (c + 1) * 16], spread, ((1,), (0,)))
        lines.append(jnp.sum(jnp.where(mine, wide, 0.0), axis=0, keepdims=True))
    lines.append(jnp.zeros((4, 1024), F32))
    coef_out[...] = jnp.concatenate(lines, axis=0).astype(BF16)


def weight_kernel(weight, plus_out, minus_out):
    plus = weight[0:1] + weight[1:2]
    minus = weight[0:1] - weight[1:2]
    plus_out[...] = jnp.broadcast_to(plus, (128, 1024)).T
    minus_out[...] = jnp.broadcast_to(minus, (128, 1024)).T


def live_row(first, parity, half):
    return (first + 2 * iota((1, half), 1) + parity <= LMAX).astype(F32)


def same_kernel(place, own, plus, turned, same):
    p, first = place[3], place[4]
    half = own.shape[1]
    wide = own[...].astype(F32) * live_row(first, p, half)
    turned_now = wide.astype(BF16).T
    turned[...] = turned_now
    scale = jnp.concatenate([plus[...]] * (half // 128), axis=1)
    same[...] = dot(turned_now, (wide * scale).astype(BF16), ((1,), (0,)))


def cross_kernel(place, turned, other, minus, same, out, scaled):
    p, first = place[3], place[4]
    half = other.shape[1]

    @pl.when(pl.program_id(0) == 0)
    def _():
        live_other = live_row(first, 1 - p, half)
        scale = jnp.concatenate([minus[...]] * (half // 128), axis=1)
        scaled[...] = (other[...].astype(F32) * live_other * scale).astype(BF16)

    cross = dot(turned[...], scaled[...], ((1,), (0,)))
    same_now = same[...]
    out[:, 0, :] = jnp.where(p == 0, same_now, cross)
    out[:, 1, :] = jnp.where(p == 0, cross, same_now)


def right_kernel(place, coef, turned, right):
    p, first, order = place[3], place[4], place[5]
    half = turned.shape[0]
    product = dot(coef[...], turned[...], ((1,), (1,)))
    sign = 1.0 - 2.0 * ((first + p + order + iota((1, half), 1) * 2) & 1).astype(F32)
    right[0] = product[0:1] + sign * product[1:2]
    right[1] = product[2:3] + sign * product[3:4]


def add_kernel(place, kept, came, normals, out):
    p, first = place[3], place[4]
    live_left = (first + 2 * iota((128, 128), 0) + p <= LMAX).astype(F32)
    gram = kept[...] + came[...]
    for q in range(2):
        live_top = (first + 2 * iota((128, 128), 1) + q <= LMAX).astype(F32)
        add = gram[:, q * 128 : (q + 1) * 128] * (live_left * live_top)
        out[:, q, :] = normals[:, q, :] + add


def whole(memory_space=pltpu.VMEM):
    return pl.BlockSpec(memory_space=memory_space)


def shards(anomaly, row_weight, panel, order_value, deg_first, sat_rows, sat_slot):
    lat_index = lax.axis_index("lat")
    parity = lax.axis_index("ord")
    orb_index = lax.axis_index("orb")
    row_count = panel.shape[2]
    half = panel.shape[4]
    row_all = row_weight.shape[1]
    z, y = lat_index // 4, lat_index % 4
    smem = whole(pltpu.SMEM)

    arrived = lax.all_to_all(panel, "lat", split_axis=1, concat_axis=2, tiled=True)

    own_order = lax.dynamic_slice_in_dim(order_value[0], lat_index, 1, 0)[0]
    place = jnp.stack([z, y, orb_index, parity, deg_first[0, 0], own_order]).astype(I32)
    local_weight = lax.dynamic_slice_in_dim(row_weight, lat_index * row_count, row_count, 1)
    packed = pl.pallas_call(
        prepare_kernel,
        out_shape=jax.ShapeDtypeStruct((64, 2176), BF16),
        in_specs=[smem] + [whole()] * 5,
        out_specs=whole(),
        scratch_shapes=[pltpu.VMEM((anomaly.shape[2], 128), BF16)] * 2,
        name="prepare",
    )(
        place,
        anomaly,
        local_weight.reshape(2 * row_count, 1),
        order_value,
        sat_rows,
        sat_slot.reshape(1, sat_slot.shape[0]),
    )
    weights = pl.pallas_call(
        weight_kernel,
        out_shape=(jax.ShapeDtypeStruct((row_all, 128), F32),) * 2,
        in_specs=[whole()],
        out_specs=(whole(),) * 2,
        name="weights",
    )
    plus, minus = weights(row_weight)

    width = packed.shape[1]
    blocks = packed.reshape(4, 16, width)
    sides = [blocks[0]]
    for e in (1, 2, 3):
        ring = [(a * 4 + b, a * 4 + (b + e) % 4) for a in range(16) for b in range(4)]
        sides.append(lax.ppermute(blocks[e], "lat", ring))
    sides = jnp.stack(sides, axis=1)
    groups = [sides[:, :, :512]]
    for f in (1, 2, 3):
        ring = [(i, (i + f) % 4) for i in range(4)]
        groups.append(lax.ppermute(sides[:, :, f * 512 : (f + 1) * 512], "orb", ring))
    packed = jnp.concatenate(groups + [sides[:, :, 2048:]], axis=2)
    columns = [[a * 4 + b for a in range(16)] for b in range(4)]
    packed = lax.all_to_all(
        packed, "lat", split_axis=0, concat_axis=0, axis_index_groups=columns, tiled=True
    )
    packed = packed.reshape(64, width)

    own_panel = arrived.reshape(row_all, half)
    other_panel = lax.ppermute(own_panel, "ord", [(0, 1), (1, 0)])
    same_call = pl.pallas_call(
        same_kernel,
        out_shape=(
            jax.ShapeDtypeStruct((half, row_all), BF16),
            jax.ShapeDtypeStruct((half, half), F32),
        ),
        in_specs=[smem] + [whole()] * 2,
        out_specs=(whole(),) * 2,
        name="same",
    )
    turned, same = same_call(place, own_panel, plus)
    cross_call = pl.pallas_call(
        cross_kernel,
        grid=(half // 128,),
        out_shape=jax.ShapeDtypeStruct((half, 2, half), F32),
        in_specs=[
            smem,
            pl.BlockSpec((128, row_all), lambda i: (i, 0)),
            pl.BlockSpec((row_all, half), lambda i: (0, 0)),
            pl.BlockSpec((row_all, 128), lambda i: (0, 0)),
            pl.BlockSpec((128, half), lambda i: (i, 0)),
        ],
        out_specs=pl.BlockSpec((128, 2, half), lambda i: (i, 0, 0)),
        scratch_shapes=[pltpu.VMEM((row_all, half), BF16)],
        name="cross",
    )
    normals = cross_call(place, turned, other_panel, minus, same)

    coef, sent, kept = pl.pallas_call(
        gather_kernel,
        out_shape=(
            jax.ShapeDtypeStruct((8, row_all), BF16),
            jax.ShapeDtypeStruct((128, 256), F32),
            jax.ShapeDtypeStruct((128, 256), F32),
        ),
        in_specs=[smem, whole()],
        out_specs=(whole(),) * 3,
        name="gather",
    )(place, packed)
    came = lax.ppermute(sent, "ord", [(0, 1), (1, 0)])
    right = pl.pallas_call(
        right_kernel,
        out_shape=jax.ShapeDtypeStruct((2, 1, half), F32),
        in_specs=[smem] + [whole()] * 2,
        out_specs=whole(),
        name="right",
    )(place, coef, turned)
    corner = pl.BlockSpec((128, 2, 128), lambda i: (0, 0, 0))
    gram_spec = pl.BlockSpec((128, 256), lambda i: (0, 0))
    normals = pl.pallas_call(
        add_kernel,
        grid=(1,),
        out_shape=jax.ShapeDtypeStruct((half, 2, half), F32),
        in_specs=[smem, gram_spec, gram_spec, corner],
        out_specs=corner,
        input_output_aliases={3: 0},
        name="add",
    )(place, kept, came, normals)
    return (normals[None, None, None], right[None, None])


def solution(mesh):
    in_specs = (
        P(None, "lat", None),
        P(),
        P("orb", None, "lat", "ord", None),
        P("orb", None),
        P("orb", "lat"),
        P(("lat", "ord", "orb"), None),
        P(("lat", "ord", "orb"), None),
    )
    out_specs = (P("orb", "lat", "ord", None, None, None), P("orb", "lat", None, "ord", None))

    return jax.shard_map(shards, mesh=mesh, in_specs=in_specs, out_specs=out_specs, check_vma=False)
```

```python
import math

import jax
import jax.numpy as jnp
from jax import lax
from jax.experimental import pallas as pl
from jax.experimental.pallas import tpu as pltpu
from jax.sharding import PartitionSpec as P


LMAX = 2190
F32 = jnp.float32
BF16 = jnp.bfloat16
I32 = jnp.int32
STEP = 144


def iota(shape, dim):
    return lax.broadcasted_iota(I32, shape, dim)


def dot(left, right, dims):
    return lax.dot_general(left, right, (dims, ((), ())), preferred_element_type=F32)


def turn(product, length):
    whole = jnp.floor(product * (1.0 / length))
    return (product - whole * length) * (2.0 * math.pi / length)


def prepare_kernel(place, anomaly, weight, order, rows, slot, out, table_high, table_low):
    y, x = place[1], place[2]
    length = anomaly.shape[2]
    order_pair = jnp.concatenate([order[...], order[...]], axis=1).astype(F32)
    fine = turn(iota((STEP, 128), 0).astype(F32) * order_pair, length)
    coarse_count = length // STEP
    coarse_rows = -(-coarse_count // 8) * 8
    coarse = turn(iota((coarse_rows, 128), 0).astype(F32) * (order_pair * STEP), length)
    cos_fine, sin_fine = jnp.cos(fine), jnp.sin(fine)
    cos_coarse, sin_coarse = jnp.cos(coarse), jnp.sin(coarse)
    left = iota((coarse_rows, 128), 1) < 64
    by_cos = jnp.where(left, cos_coarse, sin_coarse)
    by_sin = jnp.where(left, -sin_coarse, cos_coarse)
    for k in range(coarse_count):
        value = by_cos[k : k + 1] * cos_fine + by_sin[k : k + 1] * sin_fine
        high = value.astype(BF16)
        table_high[k * STEP : (k + 1) * STEP] = high
        table_low[k * STEP : (k + 1) * STEP] = (value - high.astype(F32)).astype(BF16)
    samples = anomaly[...].reshape(32, length)
    spectra = dot(samples, table_high[...], ((1,), (0,))) + dot(samples, table_low[...], ((1,), (0,)))
    coef = (spectra * math.sqrt(2.0 / length) * weight[...]).astype(BF16)
    at, own = iota((64, 64), 0), iota((64, 64), 1)

    def position(slot_in_group):
        side = ((slot_in_group & 3) - y) & 3
        return side * 16 + (slot_in_group >> 2)

    pick = (position(own) == at).astype(F32).astype(BF16)
    out[:, 2048:2176] = jnp.concatenate(
        [
            dot(pick, coef[:, :64], ((1,), (1,))),
            dot(pick, coef[:, 64:], ((1,), (1,))),
            jnp.zeros((64, 64), F32),
        ],
        axis=1,
    ).astype(BF16)
    col, to = iota((256, 256), 0), iota((256, 256), 1)
    apart = ((col & 1) * 128 + (col >> 1) == to).astype(F32).astype(BF16)
    split_rows = dot(rows[...], apart, ((1,), (0,))).astype(BF16)
    slot_row = jnp.broadcast_to(slot[...], (256, 256))
    slot_col = slot_row.T
    earlier = (slot_col == slot_row) & (col < to)
    rank = jnp.sum(jnp.where(earlier, 1.0, 0.0), axis=0, keepdims=True).astype(I32)
    slot_now = slot[...]
    bucket = ((((slot_now >> 6) - x) & 3) * 2 + rank) * 64 + position(slot_now & 63)
    chosen = (jnp.broadcast_to(bucket, (512, 256)) == iota((512, 256), 0)).astype(F32).astype(BF16)
    placed = dot(chosen, split_rows, ((1,), (0,))).astype(BF16)
    for q in range(8):
        out[:, q * 256 : (q + 1) * 256] = placed[q * 64 : (q + 1) * 64]


def weight_kernel(weight, plus_out, minus_out):
    plus = weight[0:1] + weight[1:2]
    minus = weight[0:1] - weight[1:2]
    plus_out[...] = jnp.broadcast_to(plus, (128, 1024)).T
    minus_out[...] = jnp.broadcast_to(minus, (128, 1024)).T


def live_row(first, parity, half):
    return (first + 2 * iota((1, half), 1) + parity <= LMAX).astype(F32)


def same_kernel(place, own, plus, turned, same):
    p, first = place[3], place[4]
    half = own.shape[1]
    wide = own[...].astype(F32) * live_row(first, p, half)
    turned_now = wide.astype(BF16).T
    turned[...] = turned_now
    scale = jnp.concatenate([plus[...]] * (half // 128), axis=1)
    same[...] = dot(turned_now, (wide * scale).astype(BF16), ((1,), (0,)))


def cross_kernel(place, turned, other, minus, same, out, scaled):
    p, first = place[3], place[4]
    half = other.shape[1]

    @pl.when(pl.program_id(0) == 0)
    def _():
        live_other = live_row(first, 1 - p, half)
        scale = jnp.concatenate([minus[...]] * (half // 128), axis=1)
        scaled[...] = (other[...].astype(F32) * live_other * scale).astype(BF16)

    cross = dot(turned[...], scaled[...], ((1,), (0,)))
    same_now = same[...]
    out[:, 0, :] = jnp.where(p == 0, same_now, cross)
    out[:, 1, :] = jnp.where(p == 0, cross, same_now)


def pack_kernel(*refs):
    out = refs[-1]
    at = 0
    for ref in refs[:-1]:
        width = ref.shape[2]
        out[:, :, at : at + width] = ref[...]
        at += width


def right_kernel(place, coef, turned, right):
    y, p, first, order = place[1], place[3], place[4], place[5]
    half, row_all = turned.shape
    index = iota((64, row_all), 0)
    source = (index & 60) + ((y - index) & 3)
    mine = source == (iota((64, row_all), 1) >> 4)
    spread = ((iota((16, row_all), 1) & 15) == iota((16, row_all), 0)).astype(F32).astype(BF16)
    lines = []
    for c in range(4):
        wide = dot(coef[:, c * 16 : (c + 1) * 16], spread, ((1,), (0,)))
        lines.append(jnp.sum(jnp.where(mine, wide, 0.0), axis=0, keepdims=True))
    lines.append(jnp.zeros((4, row_all), F32))
    terms = jnp.concatenate(lines, axis=0).astype(BF16)
    product = dot(terms, turned[...], ((1,), (1,)))
    sign = 1.0 - 2.0 * ((first + p + order + iota((1, half), 1) * 2) & 1).astype(F32)
    right[0] = product[0:1] + sign * product[1:2]
    right[1] = product[2:3] + sign * product[3:4]


def add_kernel(place, sat_own, sat_other, normals, out):
    p, first = place[3], place[4]
    parts = []
    for sat in (sat_own, sat_other):
        flat = sat[...].reshape(64, sat.shape[2])
        parts += [flat[:, c * 256 : (c + 1) * 256] for c in range(8)]
    block = jnp.concatenate(parts, axis=0)
    own = jnp.where(p == 0, block[:, :128], block[:, 128:])
    gram = dot(own, block, ((0,), (0,)))
    live_left = (first + 2 * iota((128, 128), 0) + p <= LMAX).astype(F32)
    for q in range(2):
        live_top = (first + 2 * iota((128, 128), 1) + q <= LMAX).astype(F32)
        add = gram[:, q * 128 : (q + 1) * 128] * (live_left * live_top)
        out[:, q, :] = normals[:, q, :] + add


def whole(memory_space=pltpu.VMEM):
    return pl.BlockSpec(memory_space=memory_space)


def shards(anomaly, row_weight, panel, order_value, deg_first, sat_rows, sat_slot):
    lat_index = lax.axis_index("lat")
    parity = lax.axis_index("ord")
    orb_index = lax.axis_index("orb")
    row_count = panel.shape[2]
    half = panel.shape[4]
    row_all = row_weight.shape[1]
    z, y = lat_index // 4, lat_index % 4
    smem = whole(pltpu.SMEM)

    arrived = lax.all_to_all(panel, "lat", split_axis=1, concat_axis=2, tiled=True)

    own_order = lax.dynamic_slice_in_dim(order_value[0], lat_index, 1, 0)[0]
    place = jnp.stack([z, y, orb_index, parity, deg_first[0, 0], own_order]).astype(I32)
    local_weight = lax.dynamic_slice_in_dim(row_weight, lat_index * row_count, row_count, 1)
    packed = pl.pallas_call(
        prepare_kernel,
        out_shape=jax.ShapeDtypeStruct((64, 2176), BF16),
        in_specs=[smem] + [whole()] * 5,
        out_specs=whole(),
        scratch_shapes=[pltpu.VMEM((anomaly.shape[2], 128), BF16)] * 2,
        name="prepare",
    )(
        place,
        anomaly,
        local_weight.reshape(2 * row_count, 1),
        order_value,
        sat_rows,
        sat_slot.reshape(1, sat_slot.shape[0]),
    )
    weights = pl.pallas_call(
        weight_kernel,
        out_shape=(jax.ShapeDtypeStruct((row_all, 128), F32),) * 2,
        in_specs=[whole()],
        out_specs=(whole(),) * 2,
        name="weights",
    )
    plus, minus = weights(row_weight)

    width = packed.shape[1]
    blocks = packed.reshape(4, 16, width)
    sides = [blocks[0]]
    for e in (1, 2, 3):
        ring = [(a * 4 + b, a * 4 + (b + e) % 4) for a in range(16) for b in range(4)]
        sides.append(lax.ppermute(blocks[e], "lat", ring))
    sides = jnp.stack(sides, axis=1)
    groups = [sides[:, :, :512]]
    for f in (1, 2, 3):
        ring = [(i, (i + f) % 4) for i in range(4)]
        groups.append(lax.ppermute(sides[:, :, f * 512 : (f + 1) * 512], "orb", ring))
    groups.append(sides[:, :, 2048:])
    pack = pl.pallas_call(
        pack_kernel,
        out_shape=jax.ShapeDtypeStruct((16, 4, width), BF16),
        in_specs=[whole()] * 5,
        out_specs=whole(),
        name="pack",
    )
    packed = pack(*groups)
    columns = [[a * 4 + b for a in range(16)] for b in range(4)]
    sat_own = lax.all_to_all(
        packed, "lat", split_axis=0, concat_axis=0, axis_index_groups=columns, tiled=True
    )
    sat_other = lax.ppermute(sat_own, "ord", [(0, 1), (1, 0)])

    own_panel = arrived.reshape(row_all, half)
    other_panel = lax.ppermute(own_panel, "ord", [(0, 1), (1, 0)])
    same_call = pl.pallas_call(
        same_kernel,
        out_shape=(
            jax.ShapeDtypeStruct((half, row_all), BF16),
            jax.ShapeDtypeStruct((half, half), F32),
        ),
        in_specs=[smem] + [whole()] * 2,
        out_specs=(whole(),) * 2,
        name="same",
    )
    turned, same = same_call(place, own_panel, plus)
    cross_call = pl.pallas_call(
        cross_kernel,
        grid=(half // 128,),
        out_shape=jax.ShapeDtypeStruct((half, 2, half), F32),
        in_specs=[
            smem,
            pl.BlockSpec((128, row_all), lambda i: (i, 0)),
            pl.BlockSpec((row_all, half), lambda i: (0, 0)),
            pl.BlockSpec((row_all, 128), lambda i: (0, 0)),
            pl.BlockSpec((128, half), lambda i: (i, 0)),
        ],
        out_specs=pl.BlockSpec((128, 2, half), lambda i: (i, 0, 0)),
        scratch_shapes=[pltpu.VMEM((row_all, half), BF16)],
        name="cross",
    )
    normals = cross_call(place, turned, other_panel, minus, same)

    right_call = pl.pallas_call(
        right_kernel,
        out_shape=jax.ShapeDtypeStruct((2, 1, half), F32),
        in_specs=[smem] + [whole()] * 2,
        out_specs=whole(),
        name="right",
    )
    right = right_call(place, sat_own.reshape(64, width)[:, 2048:], turned)
    corner = pl.BlockSpec((128, 2, 128), lambda i: (0, 0, 0))
    sat_spec = pl.BlockSpec((16, 4, width), lambda i: (0, 0, 0))
    normals = pl.pallas_call(
        add_kernel,
        grid=(1,),
        out_shape=jax.ShapeDtypeStruct((half, 2, half), F32),
        in_specs=[smem, sat_spec, sat_spec, corner],
        out_specs=corner,
        input_output_aliases={3: 0},
        name="add",
    )(place, sat_own, sat_other, normals)
    return (normals[None, None, None], right[None, None])


def solution(mesh):
    in_specs = (
        P(None, "lat", None),
        P(),
        P("orb", None, "lat", "ord", None),
        P("orb", None),
        P("orb", "lat"),
        P(("lat", "ord", "orb"), None),
        P(("lat", "ord", "orb"), None),
    )
    out_specs = (P("orb", "lat", "ord", None, None, None), P("orb", "lat", None, "ord", None))

    return jax.shard_map(shards, mesh=mesh, in_specs=in_specs, out_specs=out_specs, check_vma=False)
```

```python
import math

import jax
import jax.numpy as jnp
from jax import lax
from jax.experimental import pallas as pl
from jax.experimental.pallas import tpu as pltpu
from jax.sharding import PartitionSpec as P


LMAX = 2190
F32 = jnp.float32
BF16 = jnp.bfloat16
I32 = jnp.int32
STEP = 144


def iota(shape, dim):
    return lax.broadcasted_iota(I32, shape, dim)


def dot(left, right, dims):
    return lax.dot_general(left, right, (dims, ((), ())), preferred_element_type=F32)


def turn(product, length):
    whole = jnp.floor(product * (1.0 / length))
    return (product - whole * length) * (2.0 * math.pi / length)


def prepare_kernel(place, anomaly, weight, order, rows, slot, out, table_high, table_low):
    far, x = place[0], place[2]
    length = anomaly.shape[2]
    order_pair = jnp.concatenate([order[...], order[...]], axis=1).astype(F32)
    fine = turn(iota((STEP, 128), 0).astype(F32) * order_pair, length)
    coarse_count = length // STEP
    coarse_rows = -(-coarse_count // 8) * 8
    coarse = turn(iota((coarse_rows, 128), 0).astype(F32) * (order_pair * STEP), length)
    cos_fine, sin_fine = jnp.cos(fine), jnp.sin(fine)
    cos_coarse, sin_coarse = jnp.cos(coarse), jnp.sin(coarse)
    left = iota((coarse_rows, 128), 1) < 64
    by_cos = jnp.where(left, cos_coarse, sin_coarse)
    by_sin = jnp.where(left, -sin_coarse, cos_coarse)
    for k in range(coarse_count):
        value = by_cos[k : k + 1] * cos_fine + by_sin[k : k + 1] * sin_fine
        high = value.astype(BF16)
        table_high[k * STEP : (k + 1) * STEP] = high
        table_low[k * STEP : (k + 1) * STEP] = (value - high.astype(F32)).astype(BF16)
    samples = anomaly[...].reshape(32, length)
    spectra = dot(samples, table_high[...], ((1,), (0,))) + dot(samples, table_low[...], ((1,), (0,)))
    coef = (spectra * math.sqrt(2.0 / length) * weight[...]).astype(BF16)
    at, own = iota((64, 64), 0), iota((64, 64), 1)

    def position(slot_in_group):
        return (((slot_in_group >> 4) - far) & 3) * 16 + (slot_in_group & 15)

    pick = (position(own) == at).astype(F32).astype(BF16)
    out[:, 2048:2176] = jnp.concatenate(
        [
            dot(pick, coef[:, :64], ((1,), (1,))),
            dot(pick, coef[:, 64:], ((1,), (1,))),
            jnp.zeros((64, 64), F32),
        ],
        axis=1,
    ).astype(BF16)
    col, to = iota((256, 256), 0), iota((256, 256), 1)
    apart = ((col & 1) * 128 + (col >> 1) == to).astype(F32).astype(BF16)
    split_rows = dot(rows[...], apart, ((1,), (0,))).astype(BF16)
    slot_row = jnp.broadcast_to(slot[...], (256, 256))
    slot_col = slot_row.T
    earlier = (slot_col == slot_row) & (col < to)
    rank = jnp.sum(jnp.where(earlier, 1.0, 0.0), axis=0, keepdims=True).astype(I32)
    slot_now = slot[...]
    bucket = ((((slot_now >> 6) - x) & 3) * 2 + rank) * 64 + position(slot_now & 63)
    chosen = (jnp.broadcast_to(bucket, (512, 256)) == iota((512, 256), 0)).astype(F32).astype(BF16)
    placed = dot(chosen, split_rows, ((1,), (0,))).astype(BF16)
    for q in range(8):
        out[:, q * 256 : (q + 1) * 256] = placed[q * 64 : (q + 1) * 64]


def weight_kernel(weight, plus_out, minus_out):
    plus = weight[0:1] + weight[1:2]
    minus = weight[0:1] - weight[1:2]
    plus_out[...] = jnp.broadcast_to(plus, (128, 1024)).T
    minus_out[...] = jnp.broadcast_to(minus, (128, 1024)).T


def live_row(first, parity, half):
    return (first + 2 * iota((1, half), 1) + parity <= LMAX).astype(F32)


def gram_kernel(place, own, other, plus, minus, out, own_here, other_here, scaled, stage, sems):
    p, first = place[3], place[4]
    _, half = own.shape
    tiles = half // 128
    fetch = [
        pltpu.make_async_copy(own, own_here, sems.at[0]),
        pltpu.make_async_copy(other, other_here, sems.at[1]),
    ]
    for copy in fetch:
        copy.start()
    scaled_as = ((own_here, plus, p), (other_here, minus, 1 - p))
    for (here, weight, parity), copy in zip(scaled_as, fetch):
        copy.wait()
        live = live_row(first, parity, half)
        scale = jnp.concatenate([weight[...]] * tiles, axis=1)
        scaled[:, pl.ds(pl.multiple_of(parity * half, 128), half)] = (
            here[...].astype(F32) * live * scale
        ).astype(BF16)
    live = live_row(first, p, half)
    sent = []
    for k, (low, high) in enumerate(((0, 3), (3, tiles))):
        cols = slice(low * 128, high * 128)
        left = (own_here[:, cols].astype(F32) * live[:, cols]).astype(BF16).T
        block = dot(left, scaled[...], ((1,), (0,)))
        count = (high - low) * 128
        for q in range(2):
            for tile in range(tiles):
                at = q * half + tile * 128
                where = pl.ds((tile * half + low * 128) * 2 + q, count, stride=2)
                stage[where, :] = block[:, at : at + 128]
        pairs = stage.reshape(tiles, half, 2, 128)
        span = pl.ds(low * 128, count)
        for tile in range(tiles):
            copy = pltpu.make_async_copy(
                pairs.at[tile, span],
                out.at[span, :, pl.ds(tile * 128, 128)],
                sems.at[2 + k * tiles + tile],
            )
            copy.start()
            sent.append(copy)
    for copy in sent:
        copy.wait()


def pack_kernel(*refs):
    out = refs[-1]
    at = 0
    for ref in refs[:-1]:
        width = ref.shape[1]
        out[:, at : at + width] = ref[...]
        at += width


def right_kernel(place, coef, own, right):
    far, p, first, order = place[0], place[3], place[4], place[5]
    row_all, half = own.shape
    index = iota((64, row_all), 0)
    source = ((far - index) & 3) * 16 + (index >> 2)
    mine = source == (iota((64, row_all), 1) >> 4)
    spread = ((iota((16, row_all), 1) & 15) == iota((16, row_all), 0)).astype(F32).astype(BF16)
    lines = []
    for c in range(4):
        wide = dot(coef[:, c * 16 : (c + 1) * 16], spread, ((1,), (0,)))
        lines.append(jnp.sum(jnp.where(mine, wide, 0.0), axis=0, keepdims=True))
    lines.append(jnp.zeros((4, row_all), F32))
    terms = jnp.concatenate(lines, axis=0).astype(BF16)
    product = dot(terms, own[...], ((1,), (0,))) * live_row(first, p, half)
    sign = 1.0 - 2.0 * ((first + p + order + iota((1, half), 1) * 2) & 1).astype(F32)
    right[0] = product[0:1] + sign * product[1:2]
    right[1] = product[2:3] + sign * product[3:4]


def add_kernel(place, sat_own, sat_other, normals, out):
    p, first = place[3], place[4]
    parts = []
    for sat in (sat_own, sat_other):
        flat = sat[...].reshape(64, sat.shape[2])
        parts += [flat[:, c * 256 : (c + 1) * 256] for c in range(8)]
    block = jnp.concatenate(parts, axis=0)
    own = jnp.where(p == 0, block[:, :128], block[:, 128:])
    gram = dot(own, block, ((0,), (0,)))
    live_left = (first + 2 * iota((128, 128), 0) + p <= LMAX).astype(F32)
    for q in range(2):
        live_top = (first + 2 * iota((128, 128), 1) + q <= LMAX).astype(F32)
        add = gram[:, q * 128 : (q + 1) * 128] * (live_left * live_top)
        out[:, q, :] = normals[:, q, :] + add


def whole(memory_space=pltpu.VMEM):
    return pl.BlockSpec(memory_space=memory_space)


def shards(anomaly, row_weight, panel, order_value, deg_first, sat_rows, sat_slot):
    lat_index = lax.axis_index("lat")
    parity = lax.axis_index("ord")
    orb_index = lax.axis_index("orb")
    row_count = panel.shape[2]
    half = panel.shape[4]
    row_all = row_weight.shape[1]
    far = lat_index // 16
    smem = whole(pltpu.SMEM)

    arrived = lax.all_to_all(panel, "lat", split_axis=1, concat_axis=2, tiled=True)

    own_order = lax.dynamic_slice_in_dim(order_value[0], lat_index, 1, 0)[0]
    place = jnp.stack([far, lat_index % 16, orb_index, parity, deg_first[0, 0], own_order]).astype(I32)
    local_weight = lax.dynamic_slice_in_dim(row_weight, lat_index * row_count, row_count, 1)
    packed = pl.pallas_call(
        prepare_kernel,
        out_shape=jax.ShapeDtypeStruct((64, 2176), BF16),
        in_specs=[smem] + [whole()] * 5,
        out_specs=whole(),
        scratch_shapes=[pltpu.VMEM((anomaly.shape[2], 128), BF16)] * 2,
        name="prepare",
    )(
        place,
        anomaly,
        local_weight.reshape(2 * row_count, 1),
        order_value,
        sat_rows,
        sat_slot.reshape(1, sat_slot.shape[0]),
    )
    weights = pl.pallas_call(
        weight_kernel,
        out_shape=(jax.ShapeDtypeStruct((row_all, 128), F32),) * 2,
        in_specs=[whole()],
        out_specs=(whole(),) * 2,
        name="weights",
    )
    plus, minus = weights(row_weight)

    width = packed.shape[1]
    groups = [packed[:, :512]]
    for f in (1, 2, 3):
        ring = [(i, (i + f) % 4) for i in range(4)]
        groups.append(lax.ppermute(packed[:, f * 512 : (f + 1) * 512], "orb", ring))
    groups.append(packed[:, 2048:])
    pack = pl.pallas_call(
        pack_kernel,
        out_shape=jax.ShapeDtypeStruct((64, width), BF16),
        in_specs=[whole()] * 5,
        out_specs=whole(),
        name="pack",
    )
    packed = pack(*groups)
    fars = [packed[:16]]
    for h in (1, 2, 3):
        ring = [(i, (i + 16 * h) % 64) for i in range(64)]
        fars.append(lax.ppermute(packed[16 * h : 16 * (h + 1)], "lat", ring))
    blocks = [[16 * g + j for j in range(16)] for g in range(4)]
    sat_own = lax.all_to_all(
        jnp.stack(fars, axis=1),
        "lat",
        split_axis=0,
        concat_axis=0,
        axis_index_groups=blocks,
        tiled=True,
    )
    sat_other = lax.ppermute(sat_own, "ord", [(0, 1), (1, 0)])

    own_panel = arrived.reshape(row_all, half)
    other_panel = lax.ppermute(own_panel, "ord", [(0, 1), (1, 0)])
    lines = half * 2 * (half // 128)
    gram_call = pl.pallas_call(
        gram_kernel,
        out_shape=jax.ShapeDtypeStruct((half, 2, half), F32),
        in_specs=[smem, whole(pl.ANY), whole(pl.ANY), whole(), whole()],
        out_specs=whole(pl.ANY),
        scratch_shapes=[
            pltpu.VMEM((row_all, half), BF16),
            pltpu.VMEM((row_all, half), BF16),
            pltpu.VMEM((row_all, 2 * half), BF16),
            pltpu.VMEM((lines, 128), F32),
            pltpu.SemaphoreType.DMA((2 + 2 * (half // 128),)),
        ],
        name="gram",
    )
    normals = gram_call(place, own_panel, other_panel, plus, minus)
    right_call = pl.pallas_call(
        right_kernel,
        out_shape=jax.ShapeDtypeStruct((2, 1, half), F32),
        in_specs=[smem] + [whole()] * 2,
        out_specs=whole(),
        name="right",
    )
    right = right_call(place, sat_own[:, :, 2048:].reshape(64, 128), own_panel)
    corner = pl.BlockSpec((128, 2, 128), lambda i: (0, 0, 0))
    sat_spec = pl.BlockSpec((16, 4, width), lambda i: (0, 0, 0))
    normals = pl.pallas_call(
        add_kernel,
        grid=(1,),
        out_shape=jax.ShapeDtypeStruct((half, 2, half), F32),
        in_specs=[smem, sat_spec, sat_spec, corner],
        out_specs=corner,
        input_output_aliases={3: 0},
        name="add",
    )(place, sat_own, sat_other, normals)
    return (normals[None, None, None], right[None, None])


def solution(mesh):
    in_specs = (
        P(None, "lat", None),
        P(),
        P("orb", None, "lat", "ord", None),
        P("orb", None),
        P("orb", "lat"),
        P(("lat", "ord", "orb"), None),
        P(("lat", "ord", "orb"), None),
    )
    out_specs = (P("orb", "lat", "ord", None, None, None), P("orb", "lat", None, "ord", None))

    return jax.shard_map(shards, mesh=mesh, in_specs=in_specs, out_specs=out_specs, check_vma=False)
```

```python
import math

import jax
import jax.numpy as jnp
from jax import lax
from jax.experimental import pallas as pl
from jax.experimental.pallas import tpu as pltpu
from jax.sharding import PartitionSpec as P


LMAX = 2190
F32 = jnp.float32
BF16 = jnp.bfloat16
I32 = jnp.int32
STEP = 144


def iota(shape, dim):
    return lax.broadcasted_iota(I32, shape, dim)


def dot(left, right, dims):
    return lax.dot_general(left, right, (dims, ((), ())), preferred_element_type=F32)


def turn(product, length):
    whole = jnp.floor(product * (1.0 / length))
    return (product - whole * length) * (2.0 * math.pi / length)


def prepare_kernel(place, anomaly, weight, order, rows, slot, out, table_high, table_low):
    y, x = place[1], place[2]
    length = anomaly.shape[2]
    order_pair = jnp.concatenate([order[...], order[...]], axis=1).astype(F32)
    fine = turn(iota((STEP, 128), 0).astype(F32) * order_pair, length)
    coarse_count = length // STEP
    coarse_rows = -(-coarse_count // 8) * 8
    coarse = turn(iota((coarse_rows, 128), 0).astype(F32) * (order_pair * STEP), length)
    cos_fine, sin_fine = jnp.cos(fine), jnp.sin(fine)
    cos_coarse, sin_coarse = jnp.cos(coarse), jnp.sin(coarse)
    left = iota((coarse_rows, 128), 1) < 64
    by_cos = jnp.where(left, cos_coarse, sin_coarse)
    by_sin = jnp.where(left, -sin_coarse, cos_coarse)
    for k in range(coarse_count):
        value = by_cos[k : k + 1] * cos_fine + by_sin[k : k + 1] * sin_fine
        high = value.astype(BF16)
        table_high[k * STEP : (k + 1) * STEP] = high
        table_low[k * STEP : (k + 1) * STEP] = (value - high.astype(F32)).astype(BF16)
    samples = anomaly[...].reshape(32, length)
    spectra = dot(samples, table_high[...], ((1,), (0,))) + dot(samples, table_low[...], ((1,), (0,)))
    coef = (spectra * math.sqrt(2.0 / length) * weight[...]).astype(BF16)
    at, own = iota((64, 64), 0), iota((64, 64), 1)

    def position(slot_in_group):
        side = ((slot_in_group & 3) - y) & 3
        return side * 16 + (slot_in_group >> 2)

    pick = (position(own) == at).astype(F32).astype(BF16)
    out[:, 2048:2176] = jnp.concatenate(
        [
            dot(pick, coef[:, :64], ((1,), (1,))),
            dot(pick, coef[:, 64:], ((1,), (1,))),
            jnp.zeros((64, 64), F32),
        ],
        axis=1,
    ).astype(BF16)
    col, to = iota((256, 256), 0), iota((256, 256), 1)
    apart = ((col & 1) * 128 + (col >> 1) == to).astype(F32).astype(BF16)
    split_rows = dot(rows[...], apart, ((1,), (0,))).astype(BF16)
    slot_row = jnp.broadcast_to(slot[...], (256, 256))
    slot_col = slot_row.T
    earlier = (slot_col == slot_row) & (col < to)
    rank = jnp.sum(jnp.where(earlier, 1.0, 0.0), axis=0, keepdims=True).astype(I32)
    slot_now = slot[...]
    bucket = ((((slot_now >> 6) - x) & 3) * 2 + rank) * 64 + position(slot_now & 63)
    chosen = (jnp.broadcast_to(bucket, (512, 256)) == iota((512, 256), 0)).astype(F32).astype(BF16)
    placed = dot(chosen, split_rows, ((1,), (0,))).astype(BF16)
    for q in range(8):
        out[:, q * 256 : (q + 1) * 256] = placed[q * 64 : (q + 1) * 64]


def weight_kernel(weight, plus_out, minus_out):
    plus = weight[0:1] + weight[1:2]
    minus = weight[0:1] - weight[1:2]
    plus_out[...] = jnp.broadcast_to(plus, (128, 1024)).T
    minus_out[...] = jnp.broadcast_to(minus, (128, 1024)).T


def live_row(first, parity, half):
    return (first + 2 * iota((1, half), 1) + parity <= LMAX).astype(F32)


def gram_kernel(place, own, other, plus, minus, out, own_here, other_here, scaled, stage, sems):
    p, first = place[3], place[4]
    _, half = own.shape
    tiles = half // 128
    fetch = [
        pltpu.make_async_copy(own, own_here, sems.at[0]),
        pltpu.make_async_copy(other, other_here, sems.at[1]),
    ]
    for copy in fetch:
        copy.start()
    scaled_as = ((own_here, plus, p), (other_here, minus, 1 - p))
    for (here, weight, parity), copy in zip(scaled_as, fetch):
        copy.wait()
        live = live_row(first, parity, half)
        scale = jnp.concatenate([weight[...]] * tiles, axis=1)
        scaled[:, pl.ds(pl.multiple_of(parity * half, 128), half)] = (
            here[...].astype(F32) * live * scale
        ).astype(BF16)
    live = live_row(first, p, half)
    sent = []
    for k, (low, high) in enumerate(((0, 3), (3, tiles))):
        cols = slice(low * 128, high * 128)
        left = (own_here[:, cols].astype(F32) * live[:, cols]).astype(BF16).T
        block = dot(left, scaled[...], ((1,), (0,)))
        count = (high - low) * 128
        for q in range(2):
            for tile in range(tiles):
                at = q * half + tile * 128
                where = pl.ds((tile * half + low * 128) * 2 + q, count, stride=2)
                stage[where, :] = block[:, at : at + 128]
        pairs = stage.reshape(tiles, half, 2, 128)
        span = pl.ds(low * 128, count)
        for tile in range(tiles):
            copy = pltpu.make_async_copy(
                pairs.at[tile, span],
                out.at[span, :, pl.ds(tile * 128, 128)],
                sems.at[2 + k * tiles + tile],
            )
            copy.start()
            sent.append(copy)
    for copy in sent:
        copy.wait()


def pack_kernel(*refs):
    out = refs[-1]
    at = 0
    for ref in refs[:-1]:
        width = ref.shape[2]
        out[:, :, at : at + width] = ref[...]
        at += width


def right_kernel(place, coef, own, right, terms, total):
    y, p, first, order = place[1], place[3], place[4], place[5]
    rows, half = own.shape
    step = pl.program_id(0)

    @pl.when(step == 0)
    def _():
        steps = terms.shape[0]
        flat = coef[...].reshape(64, 128)
        for k in range(steps):
            index = iota((64, rows), 0)
            source = (index & 60) + ((y - index) & 3)
            mine = source == (iota((64, rows), 1) >> 4) + k * (rows // 16)
            spread = ((iota((16, rows), 1) & 15) == iota((16, rows), 0)).astype(F32).astype(BF16)
            lines = []
            for c in range(4):
                wide = dot(flat[:, c * 16 : (c + 1) * 16], spread, ((1,), (0,)))
                lines.append(jnp.sum(jnp.where(mine, wide, 0.0), axis=0, keepdims=True))
            lines.append(jnp.zeros((4, rows), F32))
            terms[k] = jnp.concatenate(lines, axis=0).astype(BF16)
        total[...] = jnp.zeros(total.shape, F32)

    total[...] += dot(terms[step], own[...], ((1,), (0,)))

    @pl.when(step == pl.num_programs(0) - 1)
    def _():
        product = total[...] * live_row(first, p, half)
        degree = first + p + order + 2 * iota((1, half), 1)
        sign = 1.0 - 2.0 * (degree & 1).astype(F32)
        right[0] = product[0:1] + sign * product[1:2]
        right[1] = product[2:3] + sign * product[3:4]


def add_kernel(place, sat_own, sat_other, normals, out):
    p, first = place[3], place[4]
    parts = []
    for sat in (sat_own, sat_other):
        flat = sat[...].reshape(64, sat.shape[2])
        parts += [flat[:, c * 256 : (c + 1) * 256] for c in range(8)]
    block = jnp.concatenate(parts, axis=0)
    own = jnp.where(p == 0, block[:, :128], block[:, 128:])
    gram = dot(own, block, ((0,), (0,)))
    live_left = (first + 2 * iota((128, 128), 0) + p <= LMAX).astype(F32)
    for q in range(2):
        live_top = (first + 2 * iota((128, 128), 1) + q <= LMAX).astype(F32)
        add = gram[:, q * 128 : (q + 1) * 128] * (live_left * live_top)
        out[:, q, :] = normals[:, q, :] + add


def whole(memory_space=pltpu.VMEM):
    return pl.BlockSpec(memory_space=memory_space)


def shards(anomaly, row_weight, panel, order_value, deg_first, sat_rows, sat_slot):
    lat_index = lax.axis_index("lat")
    parity = lax.axis_index("ord")
    orb_index = lax.axis_index("orb")
    row_count = panel.shape[2]
    half = panel.shape[4]
    row_all = row_weight.shape[1]
    z, y = lat_index // 4, lat_index % 4
    smem = whole(pltpu.SMEM)

    arrived = lax.all_to_all(panel, "lat", split_axis=1, concat_axis=2, tiled=True)

    own_order = lax.dynamic_slice_in_dim(order_value[0], lat_index, 1, 0)[0]
    place = jnp.stack([z, y, orb_index, parity, deg_first[0, 0], own_order]).astype(I32)
    local_weight = lax.dynamic_slice_in_dim(row_weight, lat_index * row_count, row_count, 1)
    packed = pl.pallas_call(
        prepare_kernel,
        out_shape=jax.ShapeDtypeStruct((64, 2176), BF16),
        in_specs=[smem] + [whole()] * 5,
        out_specs=whole(),
        scratch_shapes=[pltpu.VMEM((anomaly.shape[2], 128), BF16)] * 2,
        name="prepare",
    )(
        place,
        anomaly,
        local_weight.reshape(2 * row_count, 1),
        order_value,
        sat_rows,
        sat_slot.reshape(1, sat_slot.shape[0]),
    )
    weights = pl.pallas_call(
        weight_kernel,
        out_shape=(jax.ShapeDtypeStruct((row_all, 128), F32),) * 2,
        in_specs=[whole()],
        out_specs=(whole(),) * 2,
        name="weights",
    )
    plus, minus = weights(row_weight)

    width = packed.shape[1]
    blocks = packed.reshape(4, 16, width)
    sides = [blocks[0]]
    for e in (1, 2, 3):
        ring = [(a * 4 + b, a * 4 + (b + e) % 4) for a in range(16) for b in range(4)]
        sides.append(lax.ppermute(blocks[e], "lat", ring))
    sides = jnp.stack(sides, axis=1)
    groups = [sides[:, :, :512]]
    for f in (1, 2, 3):
        ring = [(i, (i + f) % 4) for i in range(4)]
        groups.append(lax.ppermute(sides[:, :, f * 512 : (f + 1) * 512], "orb", ring))
    groups.append(sides[:, :, 2048:])
    pack = pl.pallas_call(
        pack_kernel,
        out_shape=jax.ShapeDtypeStruct((16, 4, width), BF16),
        in_specs=[whole()] * 5,
        out_specs=whole(),
        name="pack",
    )
    packed = pack(*groups)
    columns = [[a * 4 + b for a in range(16)] for b in range(4)]
    sat_own = lax.all_to_all(
        packed, "lat", split_axis=0, concat_axis=0, axis_index_groups=columns, tiled=True
    )
    sat_other = lax.ppermute(sat_own, "ord", [(0, 1), (1, 0)])

    own_panel = arrived.reshape(row_all, half)
    other_panel = lax.ppermute(own_panel, "ord", [(0, 1), (1, 0)])
    lines = half * 2 * (half // 128)
    gram_call = pl.pallas_call(
        gram_kernel,
        out_shape=jax.ShapeDtypeStruct((half, 2, half), F32),
        in_specs=[smem, whole(pl.ANY), whole(pl.ANY), whole(), whole()],
        out_specs=whole(pl.ANY),
        scratch_shapes=[
            pltpu.VMEM((row_all, half), BF16),
            pltpu.VMEM((row_all, half), BF16),
            pltpu.VMEM((row_all, 2 * half), BF16),
            pltpu.VMEM((lines, 128), F32),
            pltpu.SemaphoreType.DMA((2 + 2 * (half // 128),)),
        ],
        name="gram",
    )
    normals = gram_call(place, own_panel, other_panel, plus, minus)
    chunk = row_all // 4
    right_call = pl.pallas_call(
        right_kernel,
        grid=(4,),
        out_shape=jax.ShapeDtypeStruct((2, 1, half), F32),
        in_specs=[
            smem,
            pl.BlockSpec((16, 4, 128), lambda i: (0, 0, 16)),
            pl.BlockSpec((chunk, half), lambda i: (i, 0)),
        ],
        out_specs=pl.BlockSpec((2, 1, half), lambda i: (0, 0, 0)),
        scratch_shapes=[pltpu.VMEM((4, 8, chunk), BF16), pltpu.VMEM((8, half), F32)],
        name="right",
    )
    right = right_call(place, sat_own, own_panel)
    corner = pl.BlockSpec((128, 2, 128), lambda i: (0, 0, 0))
    sat_spec = pl.BlockSpec((16, 4, width), lambda i: (0, 0, 0))
    normals = pl.pallas_call(
        add_kernel,
        grid=(1,),
        out_shape=jax.ShapeDtypeStruct((half, 2, half), F32),
        in_specs=[smem, sat_spec, sat_spec, corner],
        out_specs=corner,
        input_output_aliases={3: 0},
        name="add",
    )(place, sat_own, sat_other, normals)
    return (normals[None, None, None], right[None, None])


def solution(mesh):
    in_specs = (
        P(None, "lat", None),
        P(),
        P("orb", None, "lat", "ord", None),
        P("orb", None),
        P("orb", "lat"),
        P(("lat", "ord", "orb"), None),
        P(("lat", "ord", "orb"), None),
    )
    out_specs = (P("orb", "lat", "ord", None, None, None), P("orb", "lat", None, "ord", None))

    return jax.shard_map(shards, mesh=mesh, in_specs=in_specs, out_specs=out_specs, check_vma=False)
```

```python
import math

import jax
import jax.numpy as jnp
from jax import lax
from jax.experimental import pallas as pl
from jax.experimental.pallas import tpu as pltpu
from jax.sharding import PartitionSpec as P


LMAX = 2190
LEAD = 10
F32 = jnp.float32
BF16 = jnp.bfloat16
I32 = jnp.int32
STEP = 144


def iota(shape, dim):
    return lax.broadcasted_iota(I32, shape, dim)


def dot(left, right, dims):
    return lax.dot_general(left, right, (dims, ((), ())), preferred_element_type=F32)


def turn(product, length):
    whole = jnp.floor(product * (1.0 / length))
    return (product - whole * length) * (2.0 * math.pi / length)


def prepare_kernel(place, anomaly, weight, order, rows, slot, out, table_high, table_low):
    y, x = place[1], place[2]
    length = anomaly.shape[2]
    order_pair = jnp.concatenate([order[...], order[...]], axis=1).astype(F32)
    fine = turn(iota((STEP, 128), 0).astype(F32) * order_pair, length)
    coarse_count = length // STEP
    coarse_rows = -(-coarse_count // 8) * 8
    coarse = turn(iota((coarse_rows, 128), 0).astype(F32) * (order_pair * STEP), length)
    cos_fine, sin_fine = jnp.cos(fine), jnp.sin(fine)
    cos_coarse, sin_coarse = jnp.cos(coarse), jnp.sin(coarse)
    left = iota((coarse_rows, 128), 1) < 64
    by_cos = jnp.where(left, cos_coarse, sin_coarse)
    by_sin = jnp.where(left, -sin_coarse, cos_coarse)
    for k in range(coarse_count):
        value = by_cos[k : k + 1] * cos_fine + by_sin[k : k + 1] * sin_fine
        high = value.astype(BF16)
        table_high[k * STEP : (k + 1) * STEP] = high
        table_low[k * STEP : (k + 1) * STEP] = (value - high.astype(F32)).astype(BF16)
    samples = anomaly[...].reshape(32, length)
    spectra = dot(samples, table_high[...], ((1,), (0,))) + dot(samples, table_low[...], ((1,), (0,)))
    coef = (spectra * math.sqrt(2.0 / length) * weight[...]).astype(BF16)
    at, own = iota((64, 64), 0), iota((64, 64), 1)

    def position(slot_in_group):
        side = ((slot_in_group & 3) - y) & 3
        return side * 16 + (((slot_in_group >> 2) - LEAD) & 15)

    pick = (position(own) == at).astype(F32).astype(BF16)
    out[:, 2048:2176] = jnp.concatenate(
        [
            dot(pick, coef[:, :64], ((1,), (1,))),
            dot(pick, coef[:, 64:], ((1,), (1,))),
            jnp.zeros((64, 64), F32),
        ],
        axis=1,
    ).astype(BF16)
    col, to = iota((256, 256), 0), iota((256, 256), 1)
    apart = ((col & 1) * 128 + (col >> 1) == to).astype(F32).astype(BF16)
    split_rows = dot(rows[...], apart, ((1,), (0,))).astype(BF16)
    slot_row = jnp.broadcast_to(slot[...], (256, 256))
    slot_col = slot_row.T
    earlier = (slot_col == slot_row) & (col < to)
    rank = jnp.sum(jnp.where(earlier, 1.0, 0.0), axis=0, keepdims=True).astype(I32)
    slot_now = slot[...]
    bucket = ((((slot_now >> 6) - x) & 3) * 2 + rank) * 64 + position(slot_now & 63)
    chosen = (jnp.broadcast_to(bucket, (512, 256)) == iota((512, 256), 0)).astype(F32).astype(BF16)
    placed = dot(chosen, split_rows, ((1,), (0,))).astype(BF16)
    for q in range(8):
        out[:, q * 256 : (q + 1) * 256] = placed[q * 64 : (q + 1) * 64]


def weight_kernel(weight, plus_out, minus_out):
    plus = weight[0:1] + weight[1:2]
    minus = weight[0:1] - weight[1:2]
    plus_out[...] = jnp.broadcast_to(plus, (128, 1024)).T
    minus_out[...] = jnp.broadcast_to(minus, (128, 1024)).T


def live_row(first, parity, half):
    return (first + 2 * iota((1, half), 1) + parity <= LMAX).astype(F32)


def gram_kernel(place, own, other, plus, minus, out, own_here, other_here, scaled, stage, sems):
    p, first = place[3], place[4]
    _, half = own.shape
    tiles = half // 128
    fetch = [
        pltpu.make_async_copy(own, own_here, sems.at[0]),
        pltpu.make_async_copy(other, other_here, sems.at[1]),
    ]
    for copy in fetch:
        copy.start()
    scaled_as = ((own_here, plus, p), (other_here, minus, 1 - p))
    for (here, weight, parity), copy in zip(scaled_as, fetch):
        copy.wait()
        live = live_row(first, parity, half)
        scale = jnp.concatenate([weight[...]] * tiles, axis=1)
        scaled[:, pl.ds(pl.multiple_of(parity * half, 128), half)] = (
            here[...].astype(F32) * live * scale
        ).astype(BF16)
    live = live_row(first, p, half)
    sent = []
    for k, (low, high) in enumerate(((0, 3), (3, tiles))):
        cols = slice(low * 128, high * 128)
        left = (own_here[:, cols].astype(F32) * live[:, cols]).astype(BF16).T
        block = dot(left, scaled[...], ((1,), (0,)))
        count = (high - low) * 128
        for q in range(2):
            for tile in range(tiles):
                at = q * half + tile * 128
                where = pl.ds((tile * half + low * 128) * 2 + q, count, stride=2)
                stage[where, :] = block[:, at : at + 128]
        pairs = stage.reshape(tiles, half, 2, 128)
        span = pl.ds(low * 128, count)
        for tile in range(tiles):
            copy = pltpu.make_async_copy(
                pairs.at[tile, span],
                out.at[span, :, pl.ds(tile * 128, 128)],
                sems.at[2 + k * tiles + tile],
            )
            copy.start()
            sent.append(copy)
    for copy in sent:
        copy.wait()


def pack_kernel(*refs):
    out = refs[-1]
    at = 0
    for ref in refs[:-1]:
        width = ref.shape[2]
        out[:, :, at : at + width] = ref[...]
        at += width


def roll_kernel(panel, out, here, sems):
    rows = panel.shape[0]
    count = sems.shape[1]
    size = rows // count
    inward, outward = [], []
    for k in range(count):
        to = pl.ds(k * size, size)
        source = panel.at[pl.ds((rows // 16 * LEAD + k * size) % rows, size)]
        inward.append(pltpu.make_async_copy(source, here.at[to], sems.at[0, k]))
        outward.append(pltpu.make_async_copy(here.at[to], out.at[to], sems.at[1, k]))
    for copy in inward:
        copy.start()
    for arrival, copy in zip(inward, outward):
        arrival.wait()
        copy.start()
    for copy in outward:
        copy.wait()


def right_kernel(place, coef, own, right, own_here, sem):
    y, p, first, order = place[1], place[3], place[4], place[5]
    rows, half = own.shape
    fetch = pltpu.make_async_copy(own, own_here, sem)
    fetch.start()
    flat = coef[...].reshape(64, 128)
    index = iota((64, rows), 0)
    source = (index & 60) + ((y - index) & 3)
    mine = source == (iota((64, rows), 1) >> 4)
    spread = ((iota((16, rows), 1) & 15) == iota((16, rows), 0)).astype(F32).astype(BF16)
    lines = []
    for c in range(4):
        wide = dot(flat[:, c * 16 : (c + 1) * 16], spread, ((1,), (0,)))
        lines.append(jnp.sum(jnp.where(mine, wide, 0.0), axis=0, keepdims=True))
    lines.append(jnp.zeros((4, rows), F32))
    terms = jnp.concatenate(lines, axis=0).astype(BF16)
    fetch.wait()
    product = dot(terms, own_here[...], ((1,), (0,))) * live_row(first, p, half)
    sign = 1.0 - 2.0 * ((first + p + order + 2 * iota((1, half), 1)) & 1).astype(F32)
    right[0] = product[0:1] + sign * product[1:2]
    right[1] = product[2:3] + sign * product[3:4]


def add_kernel(place, sat_own, sat_other, normals, out):
    p, first = place[3], place[4]
    parts = []
    for sat in (sat_own, sat_other):
        flat = sat[...].reshape(64, sat.shape[2])
        parts += [flat[:, c * 256 : (c + 1) * 256] for c in range(8)]
    block = jnp.concatenate(parts, axis=0)
    own = jnp.where(p == 0, block[:, :128], block[:, 128:])
    gram = dot(own, block, ((0,), (0,)))
    live_left = (first + 2 * iota((128, 128), 0) + p <= LMAX).astype(F32)
    for q in range(2):
        live_top = (first + 2 * iota((128, 128), 1) + q <= LMAX).astype(F32)
        add = gram[:, q * 128 : (q + 1) * 128] * (live_left * live_top)
        out[:, q, :] = normals[:, q, :] + add


def whole(memory_space=pltpu.VMEM):
    return pl.BlockSpec(memory_space=memory_space)


def shards(anomaly, row_weight, panel, order_value, deg_first, sat_rows, sat_slot):
    lat_index = lax.axis_index("lat")
    parity = lax.axis_index("ord")
    orb_index = lax.axis_index("orb")
    row_count = panel.shape[2]
    half = panel.shape[4]
    row_all = row_weight.shape[1]
    z, y = lat_index // 4, lat_index % 4
    smem = whole(pltpu.SMEM)

    flat = (panel.shape[1] * row_count, half)
    rolled = pl.pallas_call(
        roll_kernel,
        out_shape=jax.ShapeDtypeStruct(flat, panel.dtype),
        in_specs=[whole(pl.ANY)],
        out_specs=whole(pl.ANY),
        scratch_shapes=[pltpu.VMEM(flat, panel.dtype), pltpu.SemaphoreType.DMA((2, 8))],
        name="roll",
    )(panel.reshape(flat)).reshape(panel.shape)
    arrived = lax.all_to_all(
        rolled,
        "lat",
        split_axis=1,
        concat_axis=2,
        axis_index_groups=[[(4 * LEAD + k) % 64 for k in range(64)]],
        tiled=True,
    )

    own_order = lax.dynamic_slice_in_dim(order_value[0], lat_index, 1, 0)[0]
    place = jnp.stack([z, y, orb_index, parity, deg_first[0, 0], own_order]).astype(I32)
    local_weight = lax.dynamic_slice_in_dim(row_weight, lat_index * row_count, row_count, 1)
    packed = pl.pallas_call(
        prepare_kernel,
        out_shape=jax.ShapeDtypeStruct((64, 2176), BF16),
        in_specs=[smem] + [whole()] * 5,
        out_specs=whole(),
        scratch_shapes=[pltpu.VMEM((anomaly.shape[2], 128), BF16)] * 2,
        name="prepare",
    )(
        place,
        anomaly,
        local_weight.reshape(2 * row_count, 1),
        order_value,
        sat_rows,
        sat_slot.reshape(1, sat_slot.shape[0]),
    )
    weights = pl.pallas_call(
        weight_kernel,
        out_shape=(jax.ShapeDtypeStruct((row_all, 128), F32),) * 2,
        in_specs=[whole()],
        out_specs=(whole(),) * 2,
        name="weights",
    )
    plus, minus = weights(jnp.roll(row_weight, -4 * LEAD * row_count, axis=1))

    width = packed.shape[1]
    blocks = packed.reshape(4, 16, width)
    sides = [blocks[0]]
    for e in (1, 2, 3):
        ring = [(a * 4 + b, a * 4 + (b + e) % 4) for a in range(16) for b in range(4)]
        sides.append(lax.ppermute(blocks[e], "lat", ring))
    sides = jnp.stack(sides, axis=1)
    groups = [sides[:, :, :512]]
    for f in (1, 2, 3):
        ring = [(i, (i + f) % 4) for i in range(4)]
        groups.append(lax.ppermute(sides[:, :, f * 512 : (f + 1) * 512], "orb", ring))
    groups.append(sides[:, :, 2048:])
    pack = pl.pallas_call(
        pack_kernel,
        out_shape=jax.ShapeDtypeStruct((16, 4, width), BF16),
        in_specs=[whole()] * 5,
        out_specs=whole(),
        name="pack",
    )
    packed = pack(*groups)
    columns = [[(LEAD + a) % 16 * 4 + b for a in range(16)] for b in range(4)]
    sat_own = lax.all_to_all(
        packed, "lat", split_axis=0, concat_axis=0, axis_index_groups=columns, tiled=True
    )
    sat_other = lax.ppermute(sat_own, "ord", [(0, 1), (1, 0)])

    own_panel = arrived.reshape(row_all, half)
    other_panel = lax.ppermute(own_panel, "ord", [(0, 1), (1, 0)])
    lines = half * 2 * (half // 128)
    gram_call = pl.pallas_call(
        gram_kernel,
        out_shape=jax.ShapeDtypeStruct((half, 2, half), F32),
        in_specs=[smem, whole(pl.ANY), whole(pl.ANY), whole(), whole()],
        out_specs=whole(pl.ANY),
        scratch_shapes=[
            pltpu.VMEM((row_all, half), BF16),
            pltpu.VMEM((row_all, half), BF16),
            pltpu.VMEM((row_all, 2 * half), BF16),
            pltpu.VMEM((lines, 128), F32),
            pltpu.SemaphoreType.DMA((2 + 2 * (half // 128),)),
        ],
        name="gram",
    )
    normals = gram_call(place, own_panel, other_panel, plus, minus)
    right_call = pl.pallas_call(
        right_kernel,
        grid=(1,),
        out_shape=jax.ShapeDtypeStruct((2, 1, half), F32),
        in_specs=[
            smem,
            pl.BlockSpec((16, 4, 128), lambda i: (0, 0, 16)),
            whole(pl.ANY),
        ],
        out_specs=pl.BlockSpec((2, 1, half), lambda i: (0, 0, 0)),
        scratch_shapes=[pltpu.VMEM((row_all, half), BF16), pltpu.SemaphoreType.DMA],
        name="right",
    )
    right = right_call(place, sat_own, own_panel)
    corner = pl.BlockSpec((128, 2, 128), lambda i: (0, 0, 0))
    sat_spec = pl.BlockSpec((16, 4, width), lambda i: (0, 0, 0))
    normals = pl.pallas_call(
        add_kernel,
        grid=(1,),
        out_shape=jax.ShapeDtypeStruct((half, 2, half), F32),
        in_specs=[smem, sat_spec, sat_spec, corner],
        out_specs=corner,
        input_output_aliases={3: 0},
        name="add",
    )(place, sat_own, sat_other, normals)
    return (normals[None, None, None], right[None, None])


def solution(mesh):
    in_specs = (
        P(None, "lat", None),
        P(),
        P("orb", None, "lat", "ord", None),
        P("orb", None),
        P("orb", "lat"),
        P(("lat", "ord", "orb"), None),
        P(("lat", "ord", "orb"), None),
    )
    out_specs = (P("orb", "lat", "ord", None, None, None), P("orb", "lat", None, "ord", None))

    return jax.shard_map(shards, mesh=mesh, in_specs=in_specs, out_specs=out_specs, check_vma=False)
```

```python
import math

import jax
import jax.numpy as jnp
from jax import lax
from jax.experimental import pallas as pl
from jax.experimental.pallas import tpu as pltpu
from jax.sharding import PartitionSpec as P


LMAX = 2190
LEAD = 10
SAT_LEAD = 10
F32 = jnp.float32
BF16 = jnp.bfloat16
I32 = jnp.int32
STEP = 144


def iota(shape, dim):
    return lax.broadcasted_iota(I32, shape, dim)


def dot(left, right, dims):
    return lax.dot_general(left, right, (dims, ((), ())), preferred_element_type=F32)


def turn(product, length):
    whole = jnp.floor(product * (1.0 / length))
    return (product - whole * length) * (2.0 * math.pi / length)


def prepare_kernel(place, anomaly, weight, order, rows, slot, out, table_high, table_low):
    y, x = place[1], place[2]
    length = anomaly.shape[2]
    order_pair = jnp.concatenate([order[...], order[...]], axis=1).astype(F32)
    fine = turn(iota((STEP, 128), 0).astype(F32) * order_pair, length)
    coarse_count = length // STEP
    coarse_rows = -(-coarse_count // 8) * 8
    coarse = turn(iota((coarse_rows, 128), 0).astype(F32) * (order_pair * STEP), length)
    cos_fine, sin_fine = jnp.cos(fine), jnp.sin(fine)
    cos_coarse, sin_coarse = jnp.cos(coarse), jnp.sin(coarse)
    left = iota((coarse_rows, 128), 1) < 64
    by_cos = jnp.where(left, cos_coarse, sin_coarse)
    by_sin = jnp.where(left, -sin_coarse, cos_coarse)
    for k in range(coarse_count):
        value = by_cos[k : k + 1] * cos_fine + by_sin[k : k + 1] * sin_fine
        high = value.astype(BF16)
        table_high[k * STEP : (k + 1) * STEP] = high
        table_low[k * STEP : (k + 1) * STEP] = (value - high.astype(F32)).astype(BF16)
    samples = anomaly[...].reshape(32, length)
    spectra = dot(samples, table_high[...], ((1,), (0,))) + dot(samples, table_low[...], ((1,), (0,)))
    coef = (spectra * math.sqrt(2.0 / length) * weight[...]).astype(BF16)
    at, own = iota((64, 64), 0), iota((64, 64), 1)

    def position(slot_in_group):
        side = ((slot_in_group & 3) - y) & 3
        return side * 16 + (((slot_in_group >> 2) - SAT_LEAD) & 15)

    pick = (position(own) == at).astype(F32).astype(BF16)
    out[:, 2048:2176] = jnp.concatenate(
        [
            dot(pick, coef[:, :64], ((1,), (1,))),
            dot(pick, coef[:, 64:], ((1,), (1,))),
            jnp.zeros((64, 64), F32),
        ],
        axis=1,
    ).astype(BF16)
    col, to = iota((256, 256), 0), iota((256, 256), 1)
    apart = ((col & 1) * 128 + (col >> 1) == to).astype(F32).astype(BF16)
    split_rows = dot(rows[...], apart, ((1,), (0,))).astype(BF16)
    slot_row = jnp.broadcast_to(slot[...], (256, 256))
    slot_col = slot_row.T
    earlier = (slot_col == slot_row) & (col < to)
    rank = jnp.sum(jnp.where(earlier, 1.0, 0.0), axis=0, keepdims=True).astype(I32)
    slot_now = slot[...]
    bucket = ((((slot_now >> 6) - x) & 3) * 2 + rank) * 64 + position(slot_now & 63)
    chosen = (jnp.broadcast_to(bucket, (512, 256)) == iota((512, 256), 0)).astype(F32).astype(BF16)
    placed = dot(chosen, split_rows, ((1,), (0,))).astype(BF16)
    for q in range(8):
        out[:, q * 256 : (q + 1) * 256] = placed[q * 64 : (q + 1) * 64]


def weight_kernel(weight, plus_out, minus_out):
    plus = weight[0:1] + weight[1:2]
    minus = weight[0:1] - weight[1:2]
    plus_out[...] = jnp.broadcast_to(plus, (128, 1024)).T
    minus_out[...] = jnp.broadcast_to(minus, (128, 1024)).T


def live_row(first, parity, half):
    return (first + 2 * iota((1, half), 1) + parity <= LMAX).astype(F32)


def gram_kernel(place, own, other, plus, minus, out, corner, scaled, stage, sems):
    p, first = place[3], place[4]
    _, half = own.shape
    tiles = half // 128
    for here, weight, parity in ((own, plus, p), (other, minus, 1 - p)):
        live = live_row(first, parity, half)
        scale = jnp.concatenate([weight[...]] * tiles, axis=1)
        scaled[:, pl.ds(pl.multiple_of(parity * half, 128), half)] = (
            here[...].astype(F32) * live * scale
        ).astype(BF16)
    live = live_row(first, p, half)
    sent = []
    for k, (low, high) in enumerate(((0, 3), (3, tiles))):
        cols = slice(low * 128, high * 128)
        left = (own[:, cols].astype(F32) * live[:, cols]).astype(BF16).T
        block = dot(left, scaled[...], ((1,), (0,)))
        count = (high - low) * 128
        for q in range(2):
            for tile in range(tiles):
                at = q * half + tile * 128
                where = pl.ds((tile * half + low * 128) * 2 + q, count, stride=2)
                stage[where, :] = block[:, at : at + 128]
        if low == 0:
            for q in range(2):
                corner[:, q * 128 : (q + 1) * 128] = block[:128, q * half : q * half + 128]
        pairs = stage.reshape(tiles, half, 2, 128)
        span = pl.ds(low * 128, count)
        for tile in range(tiles):
            copy = pltpu.make_async_copy(
                pairs.at[tile, span],
                out.at[span, :, pl.ds(tile * 128, 128)],
                sems.at[k * tiles + tile],
            )
            copy.start()
            sent.append(copy)
    for copy in sent:
        copy.wait()


def pack_kernel(*refs):
    out = refs[-1]
    at = 0
    for ref in refs[:-1]:
        width = ref.shape[2]
        out[:, :, at : at + width] = ref[...]
        at += width


def roll_kernel(panel, out, here, sems):
    rows = panel.shape[0]
    count = sems.shape[1]
    size = rows // count
    inward, outward = [], []
    for k in range(count):
        to = pl.ds(k * size, size)
        source = panel.at[pl.ds((rows // 16 * LEAD + k * size) % rows, size)]
        inward.append(pltpu.make_async_copy(source, here.at[to], sems.at[0, k]))
        outward.append(pltpu.make_async_copy(here.at[to], out.at[to], sems.at[1, k]))
    for copy in inward:
        copy.start()
    for arrival, copy in zip(inward, outward):
        arrival.wait()
        copy.start()
    for copy in outward:
        copy.wait()


def right_kernel(place, sat, own, right):
    y, p, first, order = place[1], place[3], place[4], place[5]
    rows, half = own.shape
    flat = sat[:, :, 2048:].reshape(64, 128)
    index = iota((64, 1), 0)
    z = (index >> 2) + (SAT_LEAD - LEAD)
    source = (z & 15) * 4 + ((y - index) & 3)
    mine = (source == (iota((64, rows), 1) >> 4)).astype(F32).astype(BF16)
    wide = dot(flat[:, :64], mine, ((0,), (0,)))
    keep = (iota((64, rows), 0) & 15) == (iota((64, rows), 1) & 15)
    narrow = jnp.where(keep, wide, 0.0).astype(BF16)
    line = ((iota((8, 64), 1) >> 4) == iota((8, 64), 0)).astype(F32).astype(BF16)
    terms = dot(line, narrow, ((1,), (0,))).astype(BF16)
    product = dot(terms, own[...], ((1,), (0,))) * live_row(first, p, half)
    sign = 1.0 - 2.0 * ((first + p + order + 2 * iota((1, half), 1)) & 1).astype(F32)
    right[0] = product[0:1] + sign * product[1:2]
    right[1] = product[2:3] + sign * product[3:4]


def add_kernel(place, sat_own, sat_other, corner, normals, out, stage, sem):
    p, first = place[3], place[4]
    parts = []
    for sat in (sat_own, sat_other):
        flat = sat[...].reshape(64, sat.shape[2])
        parts += [flat[:, c * 256 : (c + 1) * 256] for c in range(8)]
    block = jnp.concatenate(parts, axis=0)
    own = jnp.where(p == 0, block[:, :128], block[:, 128:])
    gram = dot(own, block, ((0,), (0,)))
    live_left = (first + 2 * iota((128, 128), 0) + p <= LMAX).astype(F32)
    for q in range(2):
        at = slice(q * 128, (q + 1) * 128)
        live_top = (first + 2 * iota((128, 128), 1) + q <= LMAX).astype(F32)
        stage[:, q, :] = corner[:, at] + gram[:, at] * (live_left * live_top)
    copy = pltpu.make_async_copy(stage, out.at[pl.ds(0, 128), :, pl.ds(0, 128)], sem)
    copy.start()
    copy.wait()


def whole(memory_space=pltpu.VMEM):
    return pl.BlockSpec(memory_space=memory_space)


def near(array):
    return pltpu.with_memory_space_constraint(array, pltpu.VMEM)


def shards(anomaly, row_weight, panel, order_value, deg_first, sat_rows, sat_slot):
    lat_index = lax.axis_index("lat")
    parity = lax.axis_index("ord")
    orb_index = lax.axis_index("orb")
    row_count = panel.shape[2]
    half = panel.shape[4]
    row_all = row_weight.shape[1]
    z, y = lat_index // 4, lat_index % 4
    smem = whole(pltpu.SMEM)

    flat = (panel.shape[1] * row_count, half)
    rolled = pl.pallas_call(
        roll_kernel,
        out_shape=jax.ShapeDtypeStruct(flat, panel.dtype),
        in_specs=[whole(pl.ANY)],
        out_specs=whole(pl.ANY),
        scratch_shapes=[pltpu.VMEM(flat, panel.dtype), pltpu.SemaphoreType.DMA((2, 8))],
        name="roll",
    )(panel.reshape(flat)).reshape(panel.shape)
    arrived = lax.all_to_all(
        rolled,
        "lat",
        split_axis=1,
        concat_axis=2,
        axis_index_groups=[[(4 * LEAD + k) % 64 for k in range(64)]],
        tiled=True,
    )

    own_order = lax.dynamic_slice_in_dim(order_value[0], lat_index, 1, 0)[0]
    place = jnp.stack([z, y, orb_index, parity, deg_first[0, 0], own_order]).astype(I32)
    local_weight = lax.dynamic_slice_in_dim(row_weight, lat_index * row_count, row_count, 1)
    packed = pl.pallas_call(
        prepare_kernel,
        out_shape=jax.ShapeDtypeStruct((64, 2176), BF16),
        in_specs=[smem] + [whole()] * 5,
        out_specs=whole(),
        scratch_shapes=[pltpu.VMEM((anomaly.shape[2], 128), BF16)] * 2,
        name="prepare",
    )(
        place,
        anomaly,
        local_weight.reshape(2 * row_count, 1),
        order_value,
        sat_rows,
        sat_slot.reshape(1, sat_slot.shape[0]),
    )
    weights = pl.pallas_call(
        weight_kernel,
        out_shape=(jax.ShapeDtypeStruct((row_all, 128), F32),) * 2,
        in_specs=[whole()],
        out_specs=(whole(),) * 2,
        name="weights",
    )
    plus, minus = weights(jnp.roll(row_weight, -4 * LEAD * row_count, axis=1))

    width = packed.shape[1]
    blocks = packed.reshape(4, 16, width)
    sides = [blocks[0]]
    for e in (1, 2, 3):
        ring = [(a * 4 + b, a * 4 + (b + e) % 4) for a in range(16) for b in range(4)]
        sides.append(lax.ppermute(blocks[e], "lat", ring))
    sides = jnp.stack(sides, axis=1)
    groups = [sides[:, :, :512]]
    for f in (1, 2, 3):
        ring = [(i, (i + f) % 4) for i in range(4)]
        groups.append(lax.ppermute(sides[:, :, f * 512 : (f + 1) * 512], "orb", ring))
    groups.append(sides[:, :, 2048:])
    pack = pl.pallas_call(
        pack_kernel,
        out_shape=jax.ShapeDtypeStruct((16, 4, width), BF16),
        in_specs=[whole()] * 5,
        out_specs=whole(),
        name="pack",
    )
    packed = pack(*groups)
    columns = [[(SAT_LEAD + a) % 16 * 4 + b for a in range(16)] for b in range(4)]
    sat_own = lax.all_to_all(
        packed, "lat", split_axis=0, concat_axis=0, axis_index_groups=columns, tiled=True
    )
    sat_other = lax.ppermute(sat_own, "ord", [(0, 1), (1, 0)])

    own_panel = arrived.reshape(row_all, half)
    other_panel = lax.ppermute(own_panel, "ord", [(0, 1), (1, 0)])
    lines = half * 2 * (half // 128)
    gram_call = pl.pallas_call(
        gram_kernel,
        out_shape=(
            jax.ShapeDtypeStruct((half, 2, half), F32),
            pltpu.VMEM((128, 256), F32),
        ),
        in_specs=[smem] + [whole()] * 4,
        out_specs=(whole(pl.ANY), whole()),
        scratch_shapes=[
            pltpu.VMEM((row_all, 2 * half), BF16),
            pltpu.VMEM((lines, 128), F32),
            pltpu.SemaphoreType.DMA((2 * (half // 128),)),
        ],
        name="gram",
    )
    normals, corner = gram_call(place, near(own_panel), near(other_panel), plus, minus)
    right_call = pl.pallas_call(
        right_kernel,
        out_shape=jax.ShapeDtypeStruct((2, 1, half), F32),
        in_specs=[smem] + [whole()] * 2,
        out_specs=whole(),
        name="right",
    )
    right = right_call(place, near(sat_own), near(own_panel))
    normals = pl.pallas_call(
        add_kernel,
        out_shape=jax.ShapeDtypeStruct((half, 2, half), F32),
        in_specs=[smem] + [whole()] * 3 + [whole(pl.ANY)],
        out_specs=whole(pl.ANY),
        scratch_shapes=[pltpu.VMEM((128, 2, 128), F32), pltpu.SemaphoreType.DMA],
        input_output_aliases={4: 0},
        name="add",
    )(place, near(sat_own), near(sat_other), near(corner), normals)
    return (normals[None, None, None], right[None, None])


def solution(mesh):
    in_specs = (
        P(None, "lat", None),
        P(),
        P("orb", None, "lat", "ord", None),
        P("orb", None),
        P("orb", "lat"),
        P(("lat", "ord", "orb"), None),
        P(("lat", "ord", "orb"), None),
    )
    out_specs = (P("orb", "lat", "ord", None, None, None), P("orb", "lat", None, "ord", None))

    return jax.shard_map(shards, mesh=mesh, in_specs=in_specs, out_specs=out_specs, check_vma=False)
```

```python
import math

import jax
import jax.numpy as jnp
from jax import lax
from jax.experimental import pallas as pl
from jax.experimental.pallas import tpu as pltpu
from jax.sharding import PartitionSpec as P


LMAX = 2190
LEAD = 10
SAT_LEAD = 10
F32 = jnp.float32
BF16 = jnp.bfloat16
I32 = jnp.int32
STEP = 144


def iota(shape, dim):
    return lax.broadcasted_iota(I32, shape, dim)


def dot(left, right, dims):
    return lax.dot_general(left, right, (dims, ((), ())), preferred_element_type=F32)


def turn(product, length):
    whole = jnp.floor(product * (1.0 / length))
    return (product - whole * length) * (2.0 * math.pi / length)


def prepare_kernel(place, anomaly, weight, order, rows, slot, out, table_high, table_low):
    y, x = place[1], place[2]
    length = anomaly.shape[2]
    order_pair = jnp.concatenate([order[...], order[...]], axis=1).astype(F32)
    fine = turn(iota((STEP, 128), 0).astype(F32) * order_pair, length)
    coarse_count = length // STEP
    coarse_rows = -(-coarse_count // 8) * 8
    coarse = turn(iota((coarse_rows, 128), 0).astype(F32) * (order_pair * STEP), length)
    cos_fine, sin_fine = jnp.cos(fine), jnp.sin(fine)
    cos_coarse, sin_coarse = jnp.cos(coarse), jnp.sin(coarse)
    left = iota((coarse_rows, 128), 1) < 64
    by_cos = jnp.where(left, cos_coarse, sin_coarse)
    by_sin = jnp.where(left, -sin_coarse, cos_coarse)
    for k in range(coarse_count):
        value = by_cos[k : k + 1] * cos_fine + by_sin[k : k + 1] * sin_fine
        high = value.astype(BF16)
        table_high[k * STEP : (k + 1) * STEP] = high
        table_low[k * STEP : (k + 1) * STEP] = (value - high.astype(F32)).astype(BF16)
    samples = anomaly[...].reshape(32, length)
    spectra = dot(samples, table_high[...], ((1,), (0,))) + dot(samples, table_low[...], ((1,), (0,)))
    coef = (spectra * math.sqrt(2.0 / length) * weight[...]).astype(BF16)
    at, own = iota((64, 64), 0), iota((64, 64), 1)

    def position(slot_in_group):
        side = ((slot_in_group & 3) - y) & 3
        return side * 16 + (((slot_in_group >> 2) - SAT_LEAD) & 15)

    pick = (position(own) == at).astype(F32).astype(BF16)
    out[:, 2048:2176] = jnp.concatenate(
        [
            dot(pick, coef[:, :64], ((1,), (1,))),
            dot(pick, coef[:, 64:], ((1,), (1,))),
            jnp.zeros((64, 64), F32),
        ],
        axis=1,
    ).astype(BF16)
    col, to = iota((256, 256), 0), iota((256, 256), 1)
    apart = ((col & 1) * 128 + (col >> 1) == to).astype(F32).astype(BF16)
    split_rows = dot(rows[...], apart, ((1,), (0,))).astype(BF16)
    slot_row = jnp.broadcast_to(slot[...], (256, 256))
    slot_col = slot_row.T
    earlier = (slot_col == slot_row) & (col < to)
    rank = jnp.sum(jnp.where(earlier, 1.0, 0.0), axis=0, keepdims=True).astype(I32)
    slot_now = slot[...]
    bucket = ((((slot_now >> 6) - x) & 3) * 2 + rank) * 64 + position(slot_now & 63)
    chosen = (jnp.broadcast_to(bucket, (512, 256)) == iota((512, 256), 0)).astype(F32).astype(BF16)
    placed = dot(chosen, split_rows, ((1,), (0,))).astype(BF16)
    for q in range(8):
        out[:, q * 256 : (q + 1) * 256] = placed[q * 64 : (q + 1) * 64]


def weight_kernel(weight, plus_out, minus_out):
    plus = weight[0:1] + weight[1:2]
    minus = weight[0:1] - weight[1:2]
    plus_out[...] = jnp.broadcast_to(plus, (128, 1024)).T
    minus_out[...] = jnp.broadcast_to(minus, (128, 1024)).T


def live_row(first, parity, half):
    return (first + 2 * iota((1, half), 1) + parity <= LMAX).astype(F32)


def gram_kernel(place, own, other, plus, minus, out, corner, scaled, stage, sems):
    p, first = place[3], place[4]
    _, half = own.shape
    tiles = half // 128
    for here, weight, parity in ((own, plus, p), (other, minus, 1 - p)):
        live = live_row(first, parity, half)
        scale = jnp.concatenate([weight[...]] * tiles, axis=1)
        scaled[:, pl.ds(pl.multiple_of(parity * half, 128), half)] = (
            here[...].astype(F32) * live * scale
        ).astype(BF16)
    live = live_row(first, p, half)
    sent = []
    for k, (low, high) in enumerate(((0, 3), (3, tiles))):
        cols = slice(low * 128, high * 128)
        left = (own[:, cols].astype(F32) * live[:, cols]).astype(BF16).T
        block = dot(left, scaled[...], ((1,), (0,)))
        count = (high - low) * 128
        for q in range(2):
            for tile in range(tiles):
                at = q * half + tile * 128
                where = pl.ds((tile * half + low * 128) * 2 + q, count, stride=2)
                stage[where, :] = block[:, at : at + 128]
        if low == 0:
            for q in range(2):
                corner[:, q * 128 : (q + 1) * 128] = block[:128, q * half : q * half + 128]
        pairs = stage.reshape(tiles, half, 2, 128)
        span = pl.ds(low * 128, count)
        for tile in range(tiles):
            copy = pltpu.make_async_copy(
                pairs.at[tile, span],
                out.at[span, :, pl.ds(tile * 128, 128)],
                sems.at[k * tiles + tile],
            )
            copy.start()
            sent.append(copy)
    for copy in sent:
        copy.wait()


def pack_kernel(*refs):
    out = refs[-1]
    at = 0
    for ref in refs[:-1]:
        width = ref.shape[2]
        out[:, :, at : at + width] = ref[...]
        at += width


def roll_kernel(panel, out, here, sems):
    rows = panel.shape[0]
    count = sems.shape[1]
    size = rows // count
    inward, outward = [], []
    for k in range(count):
        to = pl.ds(k * size, size)
        source = panel.at[pl.ds((rows // 16 * LEAD + k * size) % rows, size)]
        inward.append(pltpu.make_async_copy(source, here.at[to], sems.at[0, k]))
        outward.append(pltpu.make_async_copy(here.at[to], out.at[to], sems.at[1, k]))
    for copy in inward:
        copy.start()
    for arrival, copy in zip(inward, outward):
        arrival.wait()
        copy.start()
    for copy in outward:
        copy.wait()


def sat_gram(place, sat):
    p, first = place[3], place[4]
    flat = sat[...].reshape(64, sat.shape[2])
    block = jnp.concatenate([flat[:, c * 256 : (c + 1) * 256] for c in range(8)], axis=0)
    own = jnp.where(p == 0, block[:, :128], block[:, 128:])
    gram = dot(own, block, ((0,), (0,)))
    left = (first + 2 * iota((128, 256), 0) + p <= LMAX).astype(F32)
    column = iota((128, 256), 1)
    top = (first + 2 * (column & 127) + (column >> 7) <= LMAX).astype(F32)
    return gram * (left * top)


def right_kernel(place, sat, own, corner, right, partial):
    y, p, first, order = place[1], place[3], place[4], place[5]
    rows, half = own.shape
    flat = sat[:, :, 2048:].reshape(64, 128)
    index = iota((64, 1), 0)
    z = (index >> 2) + (SAT_LEAD - LEAD)
    source = (z & 15) * 4 + ((y - index) & 3)
    mine = (source == (iota((64, rows), 1) >> 4)).astype(F32).astype(BF16)
    wide = dot(flat[:, :64], mine, ((0,), (0,)))
    keep = (iota((64, rows), 0) & 15) == (iota((64, rows), 1) & 15)
    narrow = jnp.where(keep, wide, 0.0).astype(BF16)
    line = ((iota((8, 64), 1) >> 4) == iota((8, 64), 0)).astype(F32).astype(BF16)
    terms = dot(line, narrow, ((1,), (0,))).astype(BF16)
    product = dot(terms, own[...], ((1,), (0,))) * live_row(first, p, half)
    sign = 1.0 - 2.0 * ((first + p + order + 2 * iota((1, half), 1)) & 1).astype(F32)
    right[0] = product[0:1] + sign * product[1:2]
    right[1] = product[2:3] + sign * product[3:4]
    partial[...] = corner[...] + sat_gram(place, sat)


def add_kernel(place, sat, partial, right, normals, out, right_out, stage, sems):
    first_copy = pltpu.make_async_copy(right, right_out, sems.at[0])
    first_copy.start()
    total = partial[...] + sat_gram(place, sat)
    for q in range(2):
        stage[:, q, :] = total[:, q * 128 : (q + 1) * 128]
    copies = [first_copy]
    for k in range(4):
        span = pl.ds(k * 32, 32)
        copy = pltpu.make_async_copy(
            stage.at[span], out.at[span, :, pl.ds(0, 128)], sems.at[1 + k]
        )
        copy.start()
        copies.append(copy)
    for copy in copies:
        copy.wait()


def whole(memory_space=pltpu.VMEM):
    return pl.BlockSpec(memory_space=memory_space)


def near(array):
    return pltpu.with_memory_space_constraint(array, pltpu.VMEM)


def shards(anomaly, row_weight, panel, order_value, deg_first, sat_rows, sat_slot):
    lat_index = lax.axis_index("lat")
    parity = lax.axis_index("ord")
    orb_index = lax.axis_index("orb")
    row_count = panel.shape[2]
    half = panel.shape[4]
    row_all = row_weight.shape[1]
    z, y = lat_index // 4, lat_index % 4
    smem = whole(pltpu.SMEM)

    flat = (panel.shape[1] * row_count, half)
    rolled = pl.pallas_call(
        roll_kernel,
        out_shape=jax.ShapeDtypeStruct(flat, panel.dtype),
        in_specs=[whole(pl.ANY)],
        out_specs=whole(pl.ANY),
        scratch_shapes=[pltpu.VMEM(flat, panel.dtype), pltpu.SemaphoreType.DMA((2, 8))],
        name="roll",
    )(panel.reshape(flat)).reshape(panel.shape)
    arrived = lax.all_to_all(
        rolled,
        "lat",
        split_axis=1,
        concat_axis=2,
        axis_index_groups=[[(4 * LEAD + k) % 64 for k in range(64)]],
        tiled=True,
    )

    own_order = lax.dynamic_slice_in_dim(order_value[0], lat_index, 1, 0)[0]
    place = jnp.stack([z, y, orb_index, parity, deg_first[0, 0], own_order]).astype(I32)
    local_weight = lax.dynamic_slice_in_dim(row_weight, lat_index * row_count, row_count, 1)
    packed = pl.pallas_call(
        prepare_kernel,
        out_shape=jax.ShapeDtypeStruct((64, 2176), BF16),
        in_specs=[smem] + [whole()] * 5,
        out_specs=whole(),
        scratch_shapes=[pltpu.VMEM((anomaly.shape[2], 128), BF16)] * 2,
        name="prepare",
    )(
        place,
        anomaly,
        local_weight.reshape(2 * row_count, 1),
        order_value,
        sat_rows,
        sat_slot.reshape(1, sat_slot.shape[0]),
    )
    weights = pl.pallas_call(
        weight_kernel,
        out_shape=(jax.ShapeDtypeStruct((row_all, 128), F32),) * 2,
        in_specs=[whole()],
        out_specs=(whole(),) * 2,
        name="weights",
    )
    plus, minus = weights(jnp.roll(row_weight, -4 * LEAD * row_count, axis=1))

    width = packed.shape[1]
    blocks = packed.reshape(4, 16, width)
    sides = [blocks[0]]
    for e in (1, 2, 3):
        ring = [(a * 4 + b, a * 4 + (b + e) % 4) for a in range(16) for b in range(4)]
        sides.append(lax.ppermute(blocks[e], "lat", ring))
    sides = jnp.stack(sides, axis=1)
    groups = [sides[:, :, :512]]
    for f in (1, 2, 3):
        ring = [(i, (i + f) % 4) for i in range(4)]
        groups.append(lax.ppermute(sides[:, :, f * 512 : (f + 1) * 512], "orb", ring))
    groups.append(sides[:, :, 2048:])
    pack = pl.pallas_call(
        pack_kernel,
        out_shape=jax.ShapeDtypeStruct((16, 4, width), BF16),
        in_specs=[whole()] * 5,
        out_specs=whole(),
        name="pack",
    )
    packed = pack(*groups)
    columns = [[(SAT_LEAD + a) % 16 * 4 + b for a in range(16)] for b in range(4)]
    sat_own = lax.all_to_all(
        packed, "lat", split_axis=0, concat_axis=0, axis_index_groups=columns, tiled=True
    )
    sat_other = lax.ppermute(sat_own, "ord", [(0, 1), (1, 0)])

    own_panel = arrived.reshape(row_all, half)
    other_panel = lax.ppermute(own_panel, "ord", [(0, 1), (1, 0)])
    lines = half * 2 * (half // 128)
    gram_call = pl.pallas_call(
        gram_kernel,
        out_shape=(
            jax.ShapeDtypeStruct((half, 2, half), F32),
            pltpu.VMEM((128, 256), F32),
        ),
        in_specs=[smem] + [whole()] * 4,
        out_specs=(whole(pl.ANY), whole()),
        scratch_shapes=[
            pltpu.VMEM((row_all, 2 * half), BF16),
            pltpu.VMEM((lines, 128), F32),
            pltpu.SemaphoreType.DMA((2 * (half // 128),)),
        ],
        name="gram",
    )
    normals, corner = gram_call(place, near(own_panel), near(other_panel), plus, minus)
    right_call = pl.pallas_call(
        right_kernel,
        out_shape=(pltpu.VMEM((2, 1, half), F32), pltpu.VMEM((128, 256), F32)),
        in_specs=[smem] + [whole()] * 3,
        out_specs=(whole(),) * 2,
        name="right",
    )
    right, partial = right_call(place, near(sat_own), near(own_panel), near(corner))
    normals, right = pl.pallas_call(
        add_kernel,
        out_shape=(
            jax.ShapeDtypeStruct((half, 2, half), F32),
            jax.ShapeDtypeStruct((2, 1, half), F32),
        ),
        in_specs=[smem] + [whole()] * 3 + [whole(pl.ANY)],
        out_specs=(whole(pl.ANY),) * 2,
        scratch_shapes=[pltpu.VMEM((128, 2, 128), F32), pltpu.SemaphoreType.DMA((5,))],
        input_output_aliases={4: 0},
        name="add",
    )(place, near(sat_other), near(partial), near(right), normals)
    return (normals[None, None, None], right[None, None])


def solution(mesh):
    in_specs = (
        P(None, "lat", None),
        P(),
        P("orb", None, "lat", "ord", None),
        P("orb", None),
        P("orb", "lat"),
        P(("lat", "ord", "orb"), None),
        P(("lat", "ord", "orb"), None),
    )
    out_specs = (P("orb", "lat", "ord", None, None, None), P("orb", "lat", None, "ord", None))

    return jax.shard_map(shards, mesh=mesh, in_specs=in_specs, out_specs=out_specs, check_vma=False)
```
